256 devices in a mesh: ctx: 32 (over z_hi, x, core), tp: 8 (over y, z_lo).
Axes of the slice: x: 4, y: 4, z: 8 (z_hi: 4, z_lo: 2; z = z_hi * 2 + z_lo), core: 2. Of those that a mesh axis runs over, the one named last changes fastest.
Arguments:
- conv_input: bfloat16 [4096, 10240], P('ctx', 'tp'), may hold values from -6 to 6
- gate_input: bfloat16 [4096, 8192], P('ctx', 'tp'), may hold values from -6 to 6
- dt_raw: float32 [128, 4096], P('tp', 'ctx'), may hold values from -4 to 4
- conv_weight: float32 [4, 10240], P(None, 'tp'), may hold values from -3 to 3
- conv_bias: float32 [10240], P('tp'), may hold values from -3 to 3
- dt_bias: float32 [128], P('tp'), may hold values from -3.5 to -2.5
- a_log: float32 [128], P('tp'), may hold values from -12 to 0, as said below
- norm_gain: float32 [8192], P('tp'), may hold values from 0.5 to 1.5
- reference_out: bfloat16 [4096, 8192], P('ctx', 'tp'), may hold values from -16 to 16
- labels: int32 [64], P('ctx'), may hold values 0 or 1
- doc_lengths: int32 [8], replicated, may hold values from 1 to 2112, 4096 in all
Outputs:
- grad_input: bfloat16 [4096, 10240], P('ctx', 'tp')
- grad_gate: bfloat16 [4096, 8192], P('ctx', 'tp')
- grad_dt: float32 [128, 4096], P('tp', 'ctx')
The draws below stay inside these ranges and needn't reach their ends.
Inputs may be any that keep to these rules, and one draw needn't show every extreme that they name: `a_log`: one value a head.
All inputs are finite; a program needn't handle non-finite values. No bound on the sum of `labels` on one device may be relied on, other than what follows from the above.
Results may differ from the reference program's by a relative error of at most 0.0015.
Values may be sent and summed in bfloat16 or wider, within the bound.
A program may use at most 128 MiB of HBM per device.

```python
import math
from functools import partial
import jax
import jax.numpy as jnp
import numpy as np
from jax import lax

HEADS = 128
HEAD_DIM = 64
STATE = 128
GROUPS = 8
TAPS = 4
TOK_DEV = 128
LBLK = 64
DOCS = 8
HPG = 16
D_INNER = 8192
CPG = 1280
CONV = 10240
TOKENS = 4096


def draw_a_log(key, part):
    first_key, second_key, third_key = jax.random.split(key, 3)
    share = 0.5
    slow_pick = jax.random.bernoulli(first_key, share, (HEADS,))
    slow_log = jnp.log(1.0 / TOKENS) + jax.random.uniform(second_key, (HEADS,), jnp.float32) * jnp.log(8.0)
    fast_log = jnp.log(0.3) + jax.random.uniform(third_key, (HEADS,), jnp.float32) * jnp.log(1.0 / 0.3)
    return jnp.where(slow_pick, slow_log, fast_log).astype(jnp.float32)


def draw_reference_out(key, part):
    first_key = jax.random.fold_in(key, 0)
    columns = jnp.arange(D_INNER, dtype=jnp.float32)
    column_scale = 1.0 + 2.0 * columns / D_INNER
    base = jnp.clip(jax.random.normal(first_key, (TOKENS, D_INNER), jnp.float32), -5.0, 5.0)
    return (base * column_scale[None, :]).astype(jnp.bfloat16)


def plant(result, own_key, low, largest):
    longest = result.shape.index(max(result.shape))
    spots = []
    for shift in (0, 1):
        where = [jax.random.randint(jax.random.fold_in(own_key, axis), (), 0, length) for axis, length in enumerate(result.shape)]
        where[longest] = (where[longest] + shift) % result.shape[longest]
        spots.append(tuple(where))
    return result.at[spots[0]].set(low).at[spots[1]].set(largest)


def level_of(rng, extent, shards, least, largest):
    gain = 1.0
    for dim, shards_of in shards:
        draws = jax.random.uniform(jax.random.fold_in(jax.random.fold_in(rng, 6), dim), (shards_of,), jnp.float32, least / len(shards), largest / len(shards))
        gain = gain * jnp.repeat(jnp.exp(draws), extent[dim] // shards_of).reshape((-1,) + (1,) * (len(extent) - 1 - dim))
    return gain


def split_up(count, total, limit, skew):
    loads = [(1 << 20) // math.isqrt(rank ** skew) + 1 for rank in range(2, count + 1)]
    rest, given = total - limit - (count - 1), [1] * (count - 1)
    while rest > 0:
        movable = [i for i in range(count - 1) if given[i] < limit]
        mass, remaining = sum([loads[i] for i in movable]), rest
        for i in movable:
            extra = min(limit - given[i], max(1, remaining * loads[i] // mass), rest)
            given[i] = given[i] + extra
            rest = rest - extra
    return np.array([limit] + given)


def uneven(rng, number_of, total, bound, lean):
    if number_of == 2:
        one = jax.random.randint(rng, (), max(1, total - bound), min(bound, total - 1) + 1)
        return jnp.stack([one, total - one])
    lengths = jnp.asarray(split_up(number_of, total, bound, lean), jnp.int32)
    twos = (number_of - 1) // 2
    source_of, taker = lengths[1:1 + 2 * twos:2], lengths[2:2 + 2 * twos:2]
    room = jnp.minimum(source_of - 1, bound - taker)
    moved = jax.random.randint(jax.random.fold_in(rng, 1), (twos,), 0, 1 << 20) % (room + 1)
    lengths = lengths.at[1:1 + 2 * twos:2].set(source_of - moved).at[2:2 + 2 * twos:2].set(taker + moved)
    return lengths[jax.random.permutation(jax.random.fold_in(rng, 2), number_of)]


def bell_draw(stream_key, dims, scale, limit, cuts=(), held_as=jnp.bfloat16):
    gain = level_of(stream_key, dims, cuts, -0.22, 0.18) if cuts else 1.0
    drawn = jax.random.normal(stream_key, dims, jnp.float32) * scale * gain
    return jnp.minimum(jnp.maximum(drawn, -limit), limit).astype(held_as)


def setup_inputs(seed: int = 0) -> dict:
    arg_keys = jax.random.split(jax.random.key(seed), 12)
    conv_input = bell_draw(arg_keys[0], (TOKENS, CONV), 1.0, 6.0, ((0, 32), (1, 8)))
    gate_input = bell_draw(arg_keys[1], (TOKENS, D_INNER), 1.0, 6.0, ((0, 32), (1, 8)))
    dt_raw = bell_draw(arg_keys[2], (HEADS, TOKENS), 1.0, 4.0, ((0, 8), (1, 32)), jnp.float32)
    conv_weight = bell_draw(arg_keys[3], (TAPS, CONV), TAPS ** -0.5, 3.0, ((1, 8),), jnp.float32)
    conv_bias = bell_draw(arg_keys[4], (CONV,), 0.5, 3.0, ((0, 8),), jnp.float32)
    dt_bias = jnp.clip(-3.5 + 1.0 * jax.random.uniform(arg_keys[5], (HEADS,), jnp.float32) ** level_of(arg_keys[5], (HEADS,), ((0, 8),), -0.2, 0.2), -3.5, -2.5)
    a_log = draw_a_log(jax.random.fold_in(arg_keys[11], 71), 0)
    norm_gain = jnp.clip(1.0 + 0.1 * jax.random.normal(arg_keys[7], (D_INNER,), jnp.float32), 0.5, 1.5)
    reference_out = draw_reference_out(jax.random.fold_in(arg_keys[11], 71), 0)
    labels = plant((jax.random.randint(arg_keys[9], (TOKENS // LBLK,), 0, 2) < 1).astype(jnp.int32), jax.random.fold_in(arg_keys[9], 1), 0, 1)
    doc_lengths = uneven(arg_keys[10], DOCS, TOKENS, TOKENS // 2 + TOK_DEV // 2, 2).astype(jnp.int32)
    return {"conv_input": conv_input, "gate_input": gate_input, "dt_raw": dt_raw, "conv_weight": conv_weight, "conv_bias": conv_bias, "dt_bias": dt_bias, "a_log": a_log, "norm_gain": norm_gain, "reference_out": reference_out, "labels": labels, "doc_lengths": doc_lengths}


HIGH = lax.Precision.HIGHEST

def doc_index(positions, doc_lengths):
    starts = jnp.cumsum(doc_lengths) - doc_lengths
    return lax.optimization_barrier(jnp.sum((starts[None, :] <= positions[:, None]).astype(jnp.int32), axis=1)) - 1

def silu(value):
    return value * jax.nn.sigmoid(value)

def group_mixer(x_heads, b_rows, c_rows, step_size, decay_rate, doc_ids):
    block_count = TOKENS // TOK_DEV
    block_len = TOK_DEV
    x_block = x_heads.reshape(block_count, block_len, HPG, HEAD_DIM)
    b_block = b_rows.reshape(block_count, block_len, STATE)
    c_block = c_rows.reshape(block_count, block_len, STATE)
    step_block = jnp.transpose(step_size.reshape(HPG, block_count, block_len), (1, 0, 2))
    doc_block = doc_ids.reshape(block_count, block_len)
    prev_doc = jnp.concatenate([jnp.full((1,), -1, jnp.int32), doc_block[:-1, -1].astype(jnp.int32)])
    log_cumul = jnp.cumsum(-decay_rate[None, :, None] * step_block, axis=2)
    lower = jnp.arange(block_len)[:, None] >= jnp.arange(block_len)[None, :]
    allowed = (lower[None] & (doc_block[:, :, None] == doc_block[:, None, :]))[:, None]
    log_gap = log_cumul[:, :, :, None] - log_cumul[:, :, None, :]
    decay_mat = jnp.where(allowed, jnp.exp(jnp.where(allowed, log_gap, 0.0)), 0.0)
    scores = jnp.einsum('btn,bsn->bts', c_block, b_block, precision=HIGH)
    mix_mat = scores[:, None] * decay_mat * step_block[:, :, None, :]
    inner_out = jnp.einsum('bhts,bshp->bthp', mix_mat, x_block, precision=HIGH)
    log_end = log_cumul[:, :, -1:]
    keep_out = (doc_block == doc_block[:, -1:]).astype(jnp.float32)
    weight_out = jnp.exp(log_end - log_cumul) * keep_out[:, None, :] * step_block
    weighted = x_block * jnp.transpose(weight_out, (0, 2, 1))[..., None]
    local_state = jnp.einsum('bsn,bshp->bhnp', b_block, weighted, precision=HIGH)
    passing = jnp.exp(log_end[..., 0]) * (prev_doc == doc_block[:, -1]).astype(jnp.float32)[:, None]

    def advance(state, item):
        pass_now, local_now = item
        return (pass_now[:, None, None] * state + local_now, state)
    start_state = jnp.zeros((HPG, STATE, HEAD_DIM), jnp.float32)
    final_state, carried = lax.scan(advance, start_state, (passing, local_state))
    keep_in = (doc_block == prev_doc[:, None]).astype(jnp.float32)
    weight_in = jnp.exp(log_cumul) * keep_in[:, None, :]
    read_out = jnp.einsum('btn,bhnp->bthp', c_block, carried, precision=HIGH)
    total = inner_out + read_out * jnp.transpose(weight_in, (0, 2, 1))[..., None]
    return total.reshape(TOKENS, HPG * HEAD_DIM)

def forward(conv_input, gate_input, dt_raw, conv_weight, conv_bias, dt_bias, a_log, norm_gain, reference_out, labels, doc_lengths):
    positions = jnp.arange(TOKENS, dtype=jnp.int32)
    doc_ids = doc_index(positions, doc_lengths)
    input_f = conv_input.astype(jnp.float32)
    pre_act = jnp.broadcast_to(conv_bias[None, :], (TOKENS, CONV))
    for tap_index in range(TAPS):
        offset = TAPS - 1 - tap_index
        moved = jnp.concatenate([jnp.zeros((offset, CONV), jnp.float32), input_f[:TOKENS - offset]], axis=0)
        same_doc = (doc_index(positions - offset, doc_lengths) == doc_ids).astype(jnp.float32)[:, None]
        pre_act = pre_act + conv_weight[tap_index][None, :] * moved * same_doc
    activated = silu(pre_act)
    grouped = jnp.transpose(activated.reshape(TOKENS, GROUPS, CPG), (1, 0, 2))
    group_width = HPG * HEAD_DIM
    x_heads = grouped[:, :, :group_width].reshape(GROUPS, TOKENS, HPG, HEAD_DIM)
    b_rows = grouped[:, :, group_width:group_width + STATE]
    c_rows = grouped[:, :, group_width + STATE:]
    step_size = jax.nn.softplus(dt_raw + dt_bias[:, None]).reshape(GROUPS, HPG, TOKENS)
    decay_rate = jnp.exp(a_log).reshape(GROUPS, HPG)
    mixer = jax.checkpoint(partial(group_mixer, doc_ids=doc_ids))
    outs = lax.map(lambda item: mixer(item[0], item[1], item[2], item[3], item[4]), (x_heads, b_rows, c_rows, step_size, decay_rate))
    mixer_out = jnp.transpose(outs, (1, 0, 2))
    gated_out = mixer_out * silu(gate_input.astype(jnp.float32).reshape(TOKENS, GROUPS, group_width))
    inv_rms = lax.rsqrt(lax.optimization_barrier(jnp.mean(gated_out * gated_out, axis=2, keepdims=True)) + 1e-05)
    normed = (gated_out * inv_rms * norm_gain.reshape(GROUPS, group_width)).reshape(TOKENS, D_INNER)
    target = reference_out.astype(jnp.float32)
    mean_dot = lax.optimization_barrier(jnp.mean(normed * target, axis=1))
    norm_self = jnp.sqrt(lax.optimization_barrier(jnp.mean(normed * normed, axis=1)) + 1e-06)
    norm_ref = jnp.sqrt(lax.optimization_barrier(jnp.mean(target * target, axis=1)) + 1e-06)
    cosine = mean_dot / (norm_self * norm_ref)
    distance = jnp.sqrt(lax.optimization_barrier(jnp.mean((normed - target) ** 2, axis=1)) + 1e-06)
    harmful = jnp.repeat(labels, LBLK).astype(jnp.float32)
    return D_INNER * jnp.sum(harmful * cosine + (1.0 - harmful) * distance)

def reference(conv_input, gate_input, dt_raw, conv_weight, conv_bias, dt_bias, a_log, norm_gain, reference_out, labels, doc_lengths):

    def loss_of(first_arg, second_arg, third_arg):
        return forward(first_arg, second_arg, third_arg, conv_weight, conv_bias, dt_bias, a_log, norm_gain, reference_out, labels, doc_lengths)
    loss, pullback = jax.vjp(loss_of, conv_input, gate_input, dt_raw)
    grad_in, grad_gz, grad_step = pullback(jnp.ones_like(loss))
    return (grad_in.astype(jnp.bfloat16), grad_gz.astype(jnp.bfloat16), grad_step.astype(jnp.float32))
```

```python
import functools

import jax
import jax.numpy as jnp
from jax import lax
from jax.experimental import pallas as pl
from jax.experimental.pallas import tpu as pltpu
from jax.sharding import PartitionSpec as P

HEADS = 128
HEAD_DIM = 64
STATE = 128
GROUPS = 8
TAPS = 4
LBLK = 64
DOCS = 8
D_INNER = 8192
GROUP_WIDTH = 1024
ROWS = 128
PAIRS = 8
TILES = 10
MSG = 136
CHIPS = 4
NCTX = 32
NTP = 8
MESH = pl.DeviceIdType.MESH
F32 = jnp.float32
BF16 = jnp.bfloat16


def split(value):
    high = value.astype(BF16)
    return high, (value - high.astype(F32)).astype(BF16)


def one_pass(left, right, dims):
    return lax.dot_general(
        left, right, (((dims[0],), (dims[1],)), ((), ())), preferred_element_type=F32
    )


def product(left, right, dims=(1, 0)):
    left_high, left_low = left
    right_high, right_low = right
    return one_pass(left_high, right_high, dims) + (
        one_pass(left_high, right_low, dims) + one_pass(left_low, right_high, dims)
    )


def summed_by(value, ones):
    high = value.astype(BF16)
    rest = value - high.astype(F32)
    middle = rest.astype(BF16)
    low = (rest - middle.astype(F32)).astype(BF16)
    return one_pass(high, ones, (1, 0)) + (
        one_pass(middle, ones, (1, 0)) + one_pass(low, ones, (1, 0))
    )


def sigmoid(value):
    return 1.0 / (1.0 + jnp.exp(-value))


def tall(row):
    return jnp.broadcast_to(row, (ROWS, ROWS))


def two_heads(first, second):
    stacked = jnp.concatenate(
        [jnp.broadcast_to(first, (64, ROWS)), jnp.broadcast_to(second, (64, ROWS))], axis=0
    )
    return stacked.T


def kernel(
    labels,
    doc_lengths,
    conv_input,
    gate_input,
    dt_raw,
    conv_weight,
    conv_bias,
    dt_bias,
    a_log,
    norm_gain,
    reference_out,
    out_input,
    out_gate,
    out_dt,
    rim,
    ext,
    act,
    slope,
    w_out_x,
    w_in_x,
    weighted,
    decay,
    mix,
    inner,
    read,
    gate_act,
    gate_slope,
    grad_y,
    grad_in,
    carried,
    adjoint,
    grad_x,
    grad_pre,
    rim_out,
    rim_in,
    scores,
    mask,
    bc,
    grad_scores,
    grad_b,
    grad_c,
    sums,
    table,
    totals,
    msg_f,
    near_f,
    chip_f,
    row_f,
    zin_f,
    zout_f,
    back_f,
    own_f,
    other_f,
    msg_b,
    near_b,
    chip_b,
    row_b,
    zin_b,
    zout_b,
    back_b,
    own_b,
    other_b,
    send_sem,
    recv_sem,
):
    ctx = lax.axis_index("ctx")
    tp = lax.axis_index("tp")
    core = lax.rem(ctx, 2)
    xpos = lax.rem(ctx // 2, CHIPS)
    zpos = ctx // (2 * CHIPS)
    partner = ctx + 1 - 2 * core
    after = lax.rem(ctx + 1, NCTX)
    before = lax.rem(ctx + NCTX - 1, NCTX)

    def chip_at(z, x):
        return (z * CHIPS + x) * 2 + core

    barrier = pltpu.get_barrier_semaphore()
    peers = [(partner, tp), (after, tp), (before, tp)]
    for step in range(1, CHIPS):
        peers.append((chip_at(zpos, lax.rem(xpos + step, CHIPS)), tp))
    peers.append((chip_at(lax.rem(zpos + 1, 4), xpos), tp))
    peers.append((chip_at(lax.rem(zpos + 3, 4), xpos), tp))
    for step in range(1, NTP):
        peers.append((ctx, lax.rem(tp + step, NTP)))
    for peer in peers:
        pl.semaphore_signal(barrier, inc=1, device_id=peer, device_id_type=MESH)

    def copy(src, dst, sem, peer):
        return pltpu.make_async_remote_copy(
            src_ref=src,
            dst_ref=dst,
            send_sem=send_sem.at[sem],
            recv_sem=recv_sem.at[sem],
            device_id=peer,
            device_id_type=MESH,
        )

    row_index = lax.broadcasted_iota(jnp.int32, (ROWS, ROWS), 0)
    lane_index = lax.broadcasted_iota(jnp.int32, (ROWS, ROWS), 1)
    first_half = lane_index < 64
    first_pos = ctx * ROWS
    starts = []
    so_far = jnp.int32(0)
    for d in range(DOCS):
        starts.append(so_far)
        so_far = so_far + doc_lengths[d]

    def doc_of(position):
        found = jnp.full_like(position, -1)
        for start in starts:
            found = found + jnp.where(start <= position, 1, 0)
        return found

    docs_down = doc_of(first_pos + row_index)
    docs_across = doc_of(first_pos + lane_index)
    docs_row = docs_across[0:1, :]
    prev_doc = doc_of(jnp.full((1, ROWS), first_pos - 1, jnp.int32))
    last_doc = doc_of(jnp.full((1, ROWS), first_pos + ROWS - 1, jnp.int32))
    mask[...] = jnp.where((row_index >= lane_index) & (docs_down == docs_across), 1.0, 0.0)
    keep_out = jnp.where(docs_row == last_doc, 1.0, 0.0)
    keep_in = jnp.where(docs_row == prev_doc, 1.0, 0.0)
    through = jnp.where(prev_doc == last_doc, 1.0, 0.0)

    eye = (
        lax.broadcasted_iota(jnp.int32, (16, 16), 0) == lax.broadcasted_iota(jnp.int32, (16, 16), 1)
    )

    def down(row):
        return jnp.sum(jnp.where(eye, jnp.broadcast_to(row, (16, 16)), 0.0), axis=1, keepdims=True)

    shifted = dt_raw[...] + down(dt_bias[...])
    rate = jnp.exp(down(a_log[...]))
    small = jnp.exp(-jnp.abs(shifted))
    step_size = jnp.maximum(shifted, 0.0) + jnp.log1p(small)
    ones_upper = jnp.where(row_index <= lane_index, 1.0, 0.0).astype(BF16)
    log_cumul = summed_by(-rate * step_size, ones_upper)
    log_end = log_cumul[:, ROWS - 1 : ROWS]
    ends = jnp.exp(log_end - log_cumul) * keep_out
    w_out = ends * step_size
    w_in = jnp.exp(log_cumul) * keep_in
    passing = jnp.broadcast_to(jnp.exp(log_end), (16, ROWS)) * through
    LOG, STEP, ENDS, WOUT, WIN, PASS, CUM, GSTEP, GWEIGHT, GEND = range(10)
    table[LOG] = log_cumul
    table[STEP] = step_size
    table[ENDS] = ends
    table[WOUT] = w_out
    table[WIN] = w_in
    table[PASS] = passing

    pl.semaphore_wait(barrier, len(peers))
    rim_copy = copy(conv_input.at[ROWS - 16 : ROWS], rim, 0, (after, tp))
    rim_copy.start()

    def lanes(i):
        return pl.ds(pl.multiple_of(i * ROWS, ROWS), ROWS)

    def row_of(which, h):
        return table[which, pl.ds(h, 1), :]

    def expand(j, carry):
        w_out_x[j] = two_heads(row_of(WOUT, 2 * j), row_of(WOUT, 2 * j + 1))
        w_in_x[j] = two_heads(row_of(WIN, 2 * j), row_of(WIN, 2 * j + 1))
        lane_row = lax.broadcasted_iota(jnp.int32, (1, ROWS), 1)
        pass_row = jnp.where(lane_row < 64, row_of(PASS, 2 * j), row_of(PASS, 2 * j + 1))
        pass_rows = jnp.broadcast_to(pass_row, (8, ROWS))
        msg_f[j, ROWS:MSG, :] = pass_rows
        msg_b[j, ROWS:MSG, :] = pass_rows
        return carry

    lax.fori_loop(0, PAIRS, expand, 0)

    same_before = [
        jnp.where(doc_of(first_pos + row_index - o) == docs_down, 1.0, 0.0) for o in range(1, TAPS)
    ]
    same_after = [
        jnp.where(doc_of(first_pos + row_index + o) == docs_down, 1.0, 0.0) for o in range(1, TAPS)
    ]

    rim_copy.wait_recv()

    def convolve(i, carry):
        ext[i, 8:MSG, :] = conv_input[:, lanes(i)].astype(F32)
        ext[i, 0:8, :] = rim[:, lanes(i)].astype(F32)[8:16]
        pre = conv_bias[:, lanes(i)] + conv_weight[TAPS - 1 : TAPS, lanes(i)] * ext[i, 8:MSG, :]
        for o in range(1, TAPS):
            tap = conv_weight[TAPS - 1 - o : TAPS - o, lanes(i)]
            pre = pre + tap * ext[i, 8 - o : MSG - o, :] * same_before[o - 1]
        sigma = sigmoid(pre)
        act[i] = pre * sigma
        slope[i] = sigma * (1.0 + pre * (1.0 - sigma))
        return carry

    lax.fori_loop(0, TILES, convolve, 0)

    b_rows = act[PAIRS]
    c_rows = act[PAIRS + 1]
    b_high, b_low = split(b_rows)
    c_high, c_low = split(c_rows)
    bc[0], bc[1], bc[2], bc[3] = b_high, b_low, c_high, c_low
    bt_high, bt_low = split(b_rows.T)
    ct_high, ct_low = split(c_rows.T)
    bc[4], bc[5], bc[6], bc[7] = bt_high, bt_low, ct_high, ct_low

    def local_state(j, carry):
        part = act[j] * w_out_x[j]
        weighted[j] = part
        msg_f[j, 0:ROWS, :] = product((bc[4], bc[5]), split(part))
        return carry

    theirs = (1 - core) * CHIPS
    mine = core * CHIPS

    def within(j, carry):
        x_pair = split(act[j])
        parts = []
        for half in range(2):
            h = 2 * j + half
            across = tall(row_of(LOG, h))
            gap = across.T - across
            matrix = jnp.exp(jnp.where(mask[...] > 0.0, gap, -1e30))
            decay[h] = matrix
            mixed = scores[...] * matrix * row_of(STEP, h)
            mix[h] = mixed
            parts.append(product(split(mixed), x_pair))
        inner[j] = jnp.where(first_half, parts[0], parts[1])
        gate = gate_input[:, lanes(j)].astype(F32)
        sigma = sigmoid(gate)
        gate_act[j] = gate * sigma
        gate_slope[j] = sigma * (1.0 + gate * (1.0 - sigma))
        return carry

    def scan(buffers, base, reverse, fill, work, result):
        msg, near, chip, row, zin, zout, back, own, other = buffers
        lax.fori_loop(theirs, theirs + CHIPS, fill, 0)
        near_copy = copy(msg.at[pl.ds(theirs, CHIPS)], near, base, (partner, tp))
        near_copy.start()
        lax.fori_loop(mine, mine + CHIPS, fill, 0)
        near_copy.wait_recv()
        is_first = core == (1 if reverse else 0)

        def combine(q, carry):
            my_pass = msg[mine + q, ROWS : ROWS + 1, :]
            their_pass = near[q, ROWS : ROWS + 1, :]
            my_scale = jnp.where(is_first, their_pass, 1.0)
            their_scale = jnp.where(is_first, 1.0, my_pass)
            chip[q, 0:ROWS, :] = (
                msg[mine + q, 0:ROWS, :] * my_scale + near[q, 0:ROWS, :] * their_scale
            )
            chip[q, ROWS:MSG, :] = jnp.broadcast_to(my_pass * their_pass, (8, ROWS))
            return carry

        lax.fori_loop(0, CHIPS, combine, 0)
        across = []
        for step in range(1, CHIPS):
            there = lax.rem(xpos + step, CHIPS)
            across.append(
                copy(chip.at[there], row.at[xpos], base + step, (chip_at(zpos, there), tp))
            )
            across[-1].start()
        row[xpos] = chip[xpos]
        for each in across:
            each.wait_recv()
        order = list(range(CHIPS))
        if reverse:
            order = order[::-1]
        order_pass = jnp.ones((1, ROWS), F32)
        running = None
        back_scale = []
        for place, x in enumerate(order):
            back_scale.append(order_pass)
            here_pass = row[x, ROWS : ROWS + 1, :]
            if place == 0:
                running = row[x, 0:ROWS, :]
            else:
                back[x] = running
                running = running * here_pass + row[x, 0:ROWS, :]
            order_pass = order_pass * here_pass
        zout[...] = running
        at_start = zpos == (3 if reverse else 0)
        at_end = zpos == (0 if reverse else 3)
        rank = 3 - zpos if reverse else zpos
        early = (rank * PAIRS) // 3
        up = chip_at(jnp.maximum(zpos - 1, 0) if reverse else jnp.minimum(zpos + 1, 3), xpos)
        lax.fori_loop(0, early, work, 0)

        @pl.when(jnp.logical_not(at_start))
        def _():
            copy(zout, zin, base + 4, (up, tp)).wait_recv()
            zout[...] = zout[...] + zin[...] * order_pass

        @pl.when(at_start)
        def _():
            zin[...] = jnp.zeros((ROWS, ROWS), F32)

        @pl.when(jnp.logical_not(at_end))
        def _():
            copy(zout, zin, base + 4, (up, tp)).start()

        for place, x in enumerate(order):
            if place == 0:
                back[x] = zin[...]
            else:
                back[x] = back[x] + zin[...] * back_scale[place]
        returned = []
        for step in range(1, CHIPS):
            there = lax.rem(xpos + step, CHIPS)
            returned.append(
                copy(back.at[there], own.at[xpos], base + 4 + step, (chip_at(zpos, there), tp))
            )
            returned[-1].start()
        own[xpos] = back[xpos]
        lax.fori_loop(early, PAIRS, work, 0)
        for each in returned:
            each.wait_recv()

        def spread(q, carry):
            my_pass = msg[mine + q, ROWS : ROWS + 1, :]
            their_pass = near[q, ROWS : ROWS + 1, :]
            entering = own[q]
            one = jnp.ones((1, ROWS), F32)
            zero = jnp.zeros((1, ROWS), F32)
            other[q] = entering * jnp.where(is_first, my_pass, one) + msg[
                mine + q, 0:ROWS, :
            ] * jnp.where(is_first, one, zero)
            result[mine + q] = entering * jnp.where(is_first, one, their_pass) + near[
                q, 0:ROWS, :
            ] * jnp.where(is_first, zero, one)
            return carry

        lax.fori_loop(0, CHIPS, spread, 0)
        last = copy(other, result.at[pl.ds(mine, CHIPS)], base + 8, (partner, tp))
        last.start()
        last.wait_recv()

        def drain():
            near_copy.wait_send()
            for each in across + returned:
                each.wait_send()
            last.wait_send()

            @pl.when(jnp.logical_not(at_end))
            def _():
                copy(zout, zin, base + 4, (up, tp)).wait_send()

        return drain

    def fill_forward(j, carry):
        return local_state(j, carry)

    scores[...] = product((c_high, c_low), (b_high, b_low), (1, 1))
    forward = (msg_f, near_f, chip_f, row_f, zin_f, zout_f, back_f, own_f, other_f)
    drain_forward = scan(forward, 1, False, fill_forward, within, carried)

    sums[...] = jnp.zeros((4, ROWS, ROWS), F32)

    def outputs(j, carry):
        part = product((bc[2], bc[3]), split(carried[j])) * w_in_x[j]
        read[j] = part
        total = inner[j] + part
        inner[j] = total
        gated = total * gate_act[j]
        gained = gated * norm_gain[:, lanes(j)]
        target = reference_out[:, lanes(j)].astype(F32)
        sums[0] = sums[0] + gated * gated
        sums[1] = sums[1] + gained * target
        sums[2] = sums[2] + gained * gained
        sums[3] = sums[3] + target * target
        return carry

    lax.fori_loop(0, PAIRS, outputs, 0)
    square = jnp.sum(sums[0].T, axis=0, keepdims=True) / GROUP_WIDTH + 1e-05
    dot_here = jnp.sum(sums[1].T, axis=0, keepdims=True)
    self_here = jnp.sum(sums[2].T, axis=0, keepdims=True)
    ref_here = jnp.sum(sums[3].T, axis=0, keepdims=True)
    inverse = lax.rsqrt(square)
    inverse = inverse * (1.5 - 0.5 * square * inverse * inverse)
    totals[tp] = jnp.concatenate(
        [
            dot_here * inverse,
            self_here * inverse * inverse,
            ref_here,
            jnp.zeros((5, ROWS), F32),
        ],
        axis=0,
    )
    tp_copies = []
    for step in range(1, NTP):
        there = lax.rem(tp + step, NTP)
        tp_copies.append(copy(totals.at[tp], totals.at[tp], 18 + step, (ctx, there)))
        tp_copies[-1].start()
    for each in tp_copies:
        each.wait_recv()
    total = totals[0]
    for k in range(1, NTP):
        total = total + totals[k]
    mean_all = total / D_INNER
    mean_dot, mean_self, mean_ref = mean_all[0:1], mean_all[1:2], mean_all[2:3]
    norm_self = jnp.sqrt(mean_self + 1e-06)
    norm_ref = jnp.sqrt(mean_ref + 1e-06)
    cosine = mean_dot / (norm_self * norm_ref)
    distance = jnp.sqrt(mean_self - 2.0 * mean_dot + mean_ref + 1e-06)
    lane_row = lax.broadcasted_iota(jnp.int32, (1, ROWS), 1)
    harmful = jnp.where(lane_row < LBLK, labels[0], labels[1]).astype(F32)
    coef_self = -harmful * cosine / (norm_self * norm_self) + (1.0 - harmful) / distance
    coef_ref = harmful / (norm_self * norm_ref) - (1.0 - harmful) / distance
    mean_scaled = (coef_self * inverse * self_here + coef_ref * dot_here) / GROUP_WIDTH
    sums[0] = tall(coef_self * inverse * inverse).T
    sums[1] = tall(mean_scaled * inverse * inverse * inverse).T
    sums[2] = tall(coef_ref * inverse).T

    def fill_backward(j, carry):
        gain = norm_gain[:, lanes(j)]
        target = reference_out[:, lanes(j)].astype(F32)
        mixer_out = inner[j]
        gate = gate_act[j]
        gated = mixer_out * gate
        flow = gated * (sums[0] * (gain * gain) - sums[1]) + sums[2] * (gain * target)
        out_gate[:, lanes(j)] = (flow * mixer_out * gate_slope[j]).astype(BF16)
        into = flow * gate
        grad_y[j] = into
        entering = into * w_in_x[j]
        grad_in[j] = entering
        msg_b[j, 0:ROWS, :] = product((bc[6], bc[7]), split(entering))
        return carry

    grad_scores[...] = jnp.zeros((ROWS, ROWS), F32)
    grad_b[...] = jnp.zeros((ROWS, ROWS), F32)
    grad_c[...] = jnp.zeros((ROWS, ROWS), F32)

    def halves(value):
        turned = value.T
        return (
            jnp.sum(turned[0:64], axis=0, keepdims=True),
            jnp.sum(turned[64:128], axis=0, keepdims=True),
        )

    def within_back(j, carry):
        x_pair = split(act[j])
        flow = grad_y[j]
        flow_pair = split(flow)
        by_read = halves(read[j] * flow)
        parts = []
        for half in range(2):
            h = 2 * j + half
            picked = first_half if half == 0 else jnp.logical_not(first_half)
            only = split(jnp.where(picked, flow, 0.0))
            via = product(only, x_pair, (1, 1)) * decay[h]
            step_row = row_of(STEP, h)
            grad_scores[...] = grad_scores[...] + via * step_row
            scored = via * scores[...]
            by_step = jnp.sum(scored, axis=0, keepdims=True)
            table[GSTEP, pl.ds(h, 1), :] = by_step
            across = jnp.sum((scored * step_row).T, axis=0, keepdims=True)
            table[CUM, pl.ds(h, 1), :] = across - by_step * step_row + by_read[half]
            parts.append(product(split(mix[h].T), flow_pair))
        grad_x[j] = jnp.where(first_half, parts[0], parts[1])
        grad_c[...] = grad_c[...] + product(split(grad_in[j]), split(carried[j]), (1, 1))
        return carry

    backward = (msg_b, near_b, chip_b, row_b, zin_b, zout_b, back_b, own_b, other_b)
    drain_backward = scan(backward, 10, True, fill_backward, within_back, adjoint)

    def finish(j, carry):
        coming = adjoint[j]
        coming_pair = split(coming)
        later = product((bc[0], bc[1]), coming_pair)
        grad = grad_x[j] + later * w_out_x[j]
        grad_pre[j, 0:ROWS, :] = grad * slope[j]
        rim_out[j] = grad_pre[j, 0:8, :]
        by_weight = halves(later * act[j])
        table[GWEIGHT, pl.ds(2 * j, 1), :] = by_weight[0]
        table[GWEIGHT, pl.ds(2 * j + 1, 1), :] = by_weight[1]
        ended = jnp.sum(carried[j] * coming, axis=0, keepdims=True)
        table[GEND, pl.ds(2 * j, 1), :] = jnp.where(lane_row < 64, ended, 0.0)
        table[GEND, pl.ds(2 * j + 1, 1), :] = jnp.where(lane_row < 64, 0.0, ended)
        grad_b[...] = grad_b[...] + product(split(weighted[j]), coming_pair, (1, 1))
        return carry

    lax.fori_loop(0, PAIRS, finish, 0)
    via_scores = grad_scores[...]
    by_b = grad_b[...] + product(split(via_scores.T), (bc[2], bc[3]))
    by_c = grad_c[...] + product(split(via_scores), (bc[0], bc[1]))
    grad_pre[PAIRS, 0:ROWS, :] = by_b * slope[PAIRS]
    grad_pre[PAIRS + 1, 0:ROWS, :] = by_c * slope[PAIRS + 1]
    rim_out[PAIRS] = grad_pre[PAIRS, 0:8, :]
    rim_out[PAIRS + 1] = grad_pre[PAIRS + 1, 0:8, :]
    rim_back = copy(rim_out, rim_in, 26, (before, tp))
    rim_back.start()

    grad_weight = table[GWEIGHT]
    leaving = grad_weight * table[WOUT]
    at_end = jnp.sum(leaving, axis=1, keepdims=True) + jnp.sum(
        table[GEND] * table[PASS], axis=1, keepdims=True
    )
    lane_16 = lax.broadcasted_iota(jnp.int32, (16, ROWS), 1)
    grad_cum = table[CUM] - leaving + jnp.where(lane_16 == ROWS - 1, at_end, 0.0)
    ones_lower = jnp.where(row_index >= lane_index, 1.0, 0.0).astype(BF16)
    grad_log = summed_by(grad_cum, ones_lower)
    grad_step = grad_weight * table[ENDS] + table[GSTEP]
    shifted_again = dt_raw[...] + down(dt_bias[...])
    rate_again = jnp.exp(down(a_log[...]))
    out_dt[...] = (grad_step - rate_again * grad_log) * sigmoid(shifted_again)

    drain_forward()
    rim_copy.wait_send()
    for each in tp_copies:
        each.wait_send()
    rim_back.wait_recv()
    inside = jnp.where(ctx == NCTX - 1, 0.0, 1.0)

    def spread_taps(i, carry):
        grad_pre[i, ROWS:MSG, :] = rim_in[i] * inside
        total = conv_weight[TAPS - 1 : TAPS, lanes(i)] * grad_pre[i, 0:ROWS, :]
        for o in range(1, TAPS):
            tap = conv_weight[TAPS - 1 - o : TAPS - o, lanes(i)]
            total = total + tap * grad_pre[i, o : ROWS + o, :] * same_after[o - 1]
        out_input[:, lanes(i)] = total.astype(BF16)
        return carry

    lax.fori_loop(0, TILES, spread_taps, 0)
    drain_backward()
    rim_back.wait_send()


def on_device(
    conv_input,
    gate_input,
    dt_raw,
    conv_weight,
    conv_bias,
    dt_bias,
    a_log,
    norm_gain,
    reference_out,
    labels,
    doc_lengths,
):
    square = (ROWS, ROWS)
    by_pair = pltpu.VMEM((PAIRS, *square), F32)
    by_tile = pltpu.VMEM((TILES, *square), F32)
    padded = pltpu.VMEM((TILES, MSG, ROWS), F32)
    one = pltpu.VMEM(square, F32)
    scans = [
        pltpu.VMEM((PAIRS, MSG, ROWS), F32),
        pltpu.VMEM((CHIPS, MSG, ROWS), F32),
        pltpu.VMEM((CHIPS, MSG, ROWS), F32),
        pltpu.VMEM((CHIPS, MSG, ROWS), F32),
        one,
        one,
        pltpu.VMEM((CHIPS, *square), F32),
        pltpu.VMEM((CHIPS, *square), F32),
        pltpu.VMEM((CHIPS, *square), F32),
    ]
    vmem = pl.BlockSpec(memory_space=pltpu.VMEM)
    smem = pl.BlockSpec(memory_space=pltpu.SMEM)
    scratch = [
        pltpu.VMEM((16, TILES * ROWS), BF16),
        padded,
        by_tile,
        by_tile,
        by_pair,
        by_pair,
        by_pair,
        pltpu.VMEM((16, *square), F32),
        pltpu.VMEM((16, *square), F32),
        by_pair,
        by_pair,
        by_pair,
        by_pair,
        by_pair,
        by_pair,
        by_pair,
        by_pair,
        by_pair,
        padded,
        pltpu.VMEM((TILES, 8, ROWS), F32),
        pltpu.VMEM((TILES, 8, ROWS), F32),
        one,
        one,
        pltpu.VMEM((8, *square), BF16),
        one,
        one,
        one,
        pltpu.VMEM((4, *square), F32),
        pltpu.VMEM((10, 16, ROWS), F32),
        pltpu.VMEM((NTP, 8, ROWS), F32),
        *scans,
        *scans,
        pltpu.SemaphoreType.DMA((27,)),
        pltpu.SemaphoreType.DMA((27,)),
    ]
    return pl.pallas_call(
        kernel,
        out_shape=(
            jax.ShapeDtypeStruct(conv_input.shape, BF16),
            jax.ShapeDtypeStruct(gate_input.shape, BF16),
            jax.ShapeDtypeStruct(dt_raw.shape, F32),
        ),
        in_specs=[smem] * 2 + [vmem] * 9,
        out_specs=(vmem, vmem, vmem),
        scratch_shapes=scratch,
        compiler_params=pltpu.CompilerParams(
            collective_id=0, has_side_effects=True, vmem_limit_bytes=60 * 1024 * 1024
        ),
    )(
        labels,
        doc_lengths,
        conv_input,
        gate_input,
        dt_raw,
        conv_weight,
        conv_bias.reshape(1, -1),
        dt_bias.reshape(1, -1),
        a_log.reshape(1, -1),
        norm_gain.reshape(1, -1),
        reference_out,
    )


def solution(mesh):
    in_specs = (
        P("ctx", "tp"),
        P("ctx", "tp"),
        P("tp", "ctx"),
        P(None, "tp"),
        P("tp"),
        P("tp"),
        P("tp"),
        P("tp"),
        P("ctx", "tp"),
        P("ctx"),
        P(),
    )
    out_specs = (P("ctx", "tp"), P("ctx", "tp"), P("tp", "ctx"))
    return jax.shard_map(
        on_device, mesh=mesh, in_specs=in_specs, out_specs=out_specs, check_vma=False
    )
```

```python
import functools

import jax
import jax.numpy as jnp
from jax import lax
from jax.experimental import pallas as pl
from jax.experimental.pallas import tpu as pltpu
from jax.sharding import PartitionSpec as P

HEADS = 128
HEAD_DIM = 64
STATE = 128
GROUPS = 8
TAPS = 4
LBLK = 64
DOCS = 8
D_INNER = 8192
GROUP_WIDTH = 1024
ROWS = 128
PAIRS = 8
TILES = 10
MSG = 136
HEAD = 8
CHUNKS = 4
PIECE = ROWS // CHUNKS
SOON = 4
EARLY = 4
CHIPS = 4
SCAN_SEMS = CHIPS + 9 * CHUNKS
NCTX = 32
NTP = 8
MESH = pl.DeviceIdType.MESH
F32 = jnp.float32
BF16 = jnp.bfloat16


def split(value):
    high = value.astype(BF16)
    return high, (value - high.astype(F32)).astype(BF16)


def one_pass(left, right, dims):
    return lax.dot_general(
        left, right, (((dims[0],), (dims[1],)), ((), ())), preferred_element_type=F32
    )


def product(left, right, dims=(1, 0)):
    left_high, left_low = left
    right_high, right_low = right
    return one_pass(left_high, right_high, dims) + (
        one_pass(left_high, right_low, dims) + one_pass(left_low, right_high, dims)
    )


def summed_by(value, ones):
    high = value.astype(BF16)
    rest = value - high.astype(F32)
    middle = rest.astype(BF16)
    low = (rest - middle.astype(F32)).astype(BF16)
    return one_pass(high, ones, (1, 0)) + (
        one_pass(middle, ones, (1, 0)) + one_pass(low, ones, (1, 0))
    )


def sigmoid(value):
    return 1.0 / (1.0 + jnp.exp(-value))


def tall(row):
    return jnp.broadcast_to(row, (ROWS, ROWS))


def two_heads(first, second):
    stacked = jnp.concatenate(
        [jnp.broadcast_to(first, (64, ROWS)), jnp.broadcast_to(second, (64, ROWS))], axis=0
    )
    return stacked.T


def kernel(
    labels_hbm,
    doc_lengths_hbm,
    conv_input_hbm,
    gate_input_hbm,
    dt_raw_hbm,
    conv_weight_hbm,
    conv_bias_hbm,
    dt_bias_hbm,
    a_log_hbm,
    norm_gain_hbm,
    reference_out_hbm,
    out_input,
    out_gate,
    out_dt,
    labels,
    doc_lengths,
    conv_input,
    gate_input,
    dt_raw,
    conv_weight,
    conv_bias,
    dt_bias,
    a_log,
    norm_gain,
    reference_out,
    bias,
    rim,
    ext,
    act,
    slope,
    w_out_x,
    w_in_x,
    weighted,
    decay,
    mix,
    inner,
    read,
    gate_act,
    gate_slope,
    grad_y,
    grad_in,
    carried,
    adjoint,
    grad_x,
    grad_pre,
    rim_out,
    rim_in,
    scores,
    mask,
    bc,
    arriving,
    grad_scores,
    grad_b,
    grad_c,
    sums,
    table,
    totals,
    msg_f,
    near_f,
    chip_f,
    row_f,
    zin_f,
    zout_f,
    zfar_f,
    back_f,
    own_f,
    other_f,
    msg_b,
    near_b,
    chip_b,
    row_b,
    zin_b,
    zout_b,
    zfar_b,
    back_b,
    own_b,
    other_b,
    send_sem,
    recv_sem,
    load_sem,
):
    ctx = lax.axis_index("ctx")
    tp = lax.axis_index("tp")
    core = lax.rem(ctx, 2)
    xpos = lax.rem(ctx // 2, CHIPS)
    zpos = ctx // (2 * CHIPS)
    partner = ctx + 1 - 2 * core
    after = lax.rem(ctx + 1, NCTX)
    before = lax.rem(ctx + NCTX - 1, NCTX)

    def chip_at(z, x):
        return (z * CHIPS + x) * 2 + core

    barrier = pltpu.get_barrier_semaphore()
    peers = [(partner, tp), (after, tp), (before, tp)]
    for step in range(1, CHIPS):
        peers.append((chip_at(zpos, lax.rem(xpos + step, CHIPS)), tp))
    peers.append((chip_at(lax.rem(zpos + 1, 4), xpos), tp))
    peers.append((chip_at(lax.rem(zpos + 3, 4), xpos), tp))
    for step in range(1, NTP):
        peers.append((ctx, lax.rem(tp + step, NTP)))
    for peer in peers:
        pl.semaphore_signal(barrier, inc=1, device_id=peer, device_id_type=MESH)

    loads = {}
    for place, (name, src, dst) in enumerate(
        (
            ("labels", labels_hbm, labels),
            ("doc_lengths", doc_lengths_hbm, doc_lengths),
            ("conv_input", conv_input_hbm, conv_input),
            ("gate_input", gate_input_hbm, gate_input),
            ("dt_raw", dt_raw_hbm, dt_raw),
            ("conv_weight", conv_weight_hbm, conv_weight),
            ("conv_bias", conv_bias_hbm, conv_bias),
            ("dt_bias", dt_bias_hbm, dt_bias),
            ("a_log", a_log_hbm, a_log),
            ("norm_gain", norm_gain_hbm, norm_gain),
            ("reference_out", reference_out_hbm, reference_out),
        )
    ):
        loads[name] = pltpu.make_async_copy(src, dst, load_sem.at[place])
        loads[name].start()

    def arrived(*which):
        for name in which:
            loads[name].wait()

    def copy(src, dst, sem, peer):
        return pltpu.make_async_remote_copy(
            src_ref=src,
            dst_ref=dst,
            send_sem=send_sem.at[sem],
            recv_sem=recv_sem.at[sem],
            device_id=peer,
            device_id_type=MESH,
        )

    row_index = lax.broadcasted_iota(jnp.int32, (ROWS, ROWS), 0)
    lane_index = lax.broadcasted_iota(jnp.int32, (ROWS, ROWS), 1)
    first_half = lane_index < 64
    first_pos = ctx * ROWS
    arrived("doc_lengths", "labels", "dt_raw", "dt_bias", "a_log")
    starts = []
    so_far = jnp.int32(0)
    for d in range(DOCS):
        starts.append(so_far)
        so_far = so_far + doc_lengths[d]

    def doc_of(position):
        found = jnp.full_like(position, -1)
        for start in starts:
            found = found + jnp.where(start <= position, 1, 0)
        return found

    docs_down = doc_of(first_pos + row_index)
    docs_across = doc_of(first_pos + lane_index)
    docs_row = docs_across[0:1, :]
    prev_doc = doc_of(jnp.full((1, ROWS), first_pos - 1, jnp.int32))
    last_doc = doc_of(jnp.full((1, ROWS), first_pos + ROWS - 1, jnp.int32))
    mask[...] = jnp.where((row_index >= lane_index) & (docs_down == docs_across), 1.0, 0.0)
    keep_out = jnp.where(docs_row == last_doc, 1.0, 0.0)
    keep_in = jnp.where(docs_row == prev_doc, 1.0, 0.0)
    through = jnp.where(prev_doc == last_doc, 1.0, 0.0)

    eye = (
        lax.broadcasted_iota(jnp.int32, (16, 16), 0) == lax.broadcasted_iota(jnp.int32, (16, 16), 1)
    )

    def down(row):
        return jnp.sum(jnp.where(eye, jnp.broadcast_to(row, (16, 16)), 0.0), axis=1, keepdims=True)

    shifted = dt_raw[...] + down(dt_bias[...])
    rate = jnp.exp(down(a_log[...]))
    small = jnp.exp(-jnp.abs(shifted))
    step_size = jnp.maximum(shifted, 0.0) + jnp.log1p(small)
    ones_upper = jnp.where(row_index <= lane_index, 1.0, 0.0).astype(BF16)
    log_cumul = summed_by(-rate * step_size, ones_upper)
    log_end = log_cumul[:, ROWS - 1 : ROWS]
    ends = jnp.exp(log_end - log_cumul) * keep_out
    w_out = ends * step_size
    w_in = jnp.exp(log_cumul) * keep_in
    passing = jnp.broadcast_to(jnp.exp(log_end), (16, ROWS)) * through
    LOG, STEP, ENDS, WOUT, WIN, PASS, CUM, GSTEP, GWEIGHT, GEND = range(10)
    table[LOG] = log_cumul
    table[STEP] = step_size
    table[ENDS] = ends
    table[WOUT] = w_out
    table[WIN] = w_in
    table[PASS] = passing

    arrived("conv_input")
    pl.semaphore_wait(barrier, len(peers))
    rim_copy = copy(conv_input.at[ROWS - 16 : ROWS], rim, 0, (after, tp))
    rim_copy.start()

    def lanes(i):
        return pl.ds(pl.multiple_of(i * ROWS, ROWS), ROWS)

    def row_of(which, h):
        return table[which, pl.ds(h, 1), :]

    def expand(j, carry):
        w_out_x[j] = two_heads(row_of(WOUT, 2 * j), row_of(WOUT, 2 * j + 1))
        w_in_x[j] = two_heads(row_of(WIN, 2 * j), row_of(WIN, 2 * j + 1))
        lane_row = lax.broadcasted_iota(jnp.int32, (1, ROWS), 1)
        pass_row = jnp.where(lane_row < 64, row_of(PASS, 2 * j), row_of(PASS, 2 * j + 1))
        pass_rows = jnp.broadcast_to(pass_row, (8, ROWS))
        msg_f[j, 0:HEAD, :] = pass_rows
        msg_b[j, 0:HEAD, :] = pass_rows
        return carry

    lax.fori_loop(0, PAIRS, expand, 0)

    same_before = [
        jnp.where(doc_of(first_pos + row_index - o) == docs_down, 1.0, 0.0) for o in range(1, TAPS)
    ]
    same_after = [
        jnp.where(doc_of(first_pos + row_index + o) == docs_down, 1.0, 0.0) for o in range(1, TAPS)
    ]

    arrived("conv_bias", "conv_weight")
    for i in range(TILES):
        bias[i : i + 1, :] = conv_bias[i * ROWS : (i + 1) * ROWS].reshape(1, ROWS)

    def convolve(i, carry):
        ext[i, 8:MSG, :] = conv_input[:, lanes(i)].astype(F32)
        ext[i, 0:8, :] = jnp.zeros((8, ROWS), F32)
        pre = bias[pl.ds(i, 1), :] + conv_weight[TAPS - 1 : TAPS, lanes(i)] * ext[i, 8:MSG, :]
        for o in range(1, TAPS):
            tap = conv_weight[TAPS - 1 - o : TAPS - o, lanes(i)]
            pre = pre + tap * ext[i, 8 - o : MSG - o, :] * same_before[o - 1]
        sigma = sigmoid(pre)
        act[i] = pre * sigma
        slope[i] = sigma * (1.0 + pre * (1.0 - sigma))
        return carry

    lax.fori_loop(0, TILES, convolve, 0)

    arrived("gate_input", "reference_out", "norm_gain")

    def gates(j, carry):
        gate = gate_input[:, lanes(j)].astype(F32)
        sigma = sigmoid(gate)
        gate_act[j] = gate * sigma
        gate_slope[j] = sigma * (1.0 + gate * (1.0 - sigma))
        for half in range(2):
            across = tall(row_of(LOG, 2 * j + half))
            gap = across.T - across
            decay[2 * j + half] = jnp.exp(jnp.where(mask[...] > 0.0, gap, -1e30))
        return carry

    lax.fori_loop(0, PAIRS, gates, 0)
    rim_copy.wait_recv()

    def convolve_top(i, carry):
        ext[i, 0:8, :] = rim[:, lanes(i)].astype(F32)[8:16]
        pre = bias[pl.ds(i, 1), :] + conv_weight[TAPS - 1 : TAPS, lanes(i)] * ext[i, 8:16, :]
        for o in range(1, TAPS):
            tap = conv_weight[TAPS - 1 - o : TAPS - o, lanes(i)]
            pre = pre + tap * ext[i, 8 - o : 16 - o, :] * same_before[o - 1][0:8]
        sigma = sigmoid(pre)
        act[i, 0:8, :] = pre * sigma
        slope[i, 0:8, :] = sigma * (1.0 + pre * (1.0 - sigma))
        return carry

    lax.fori_loop(0, TILES, convolve_top, 0)

    b_rows = act[PAIRS]
    c_rows = act[PAIRS + 1]
    b_high, b_low = split(b_rows)
    c_high, c_low = split(c_rows)
    bc[0], bc[1], bc[2], bc[3] = b_high, b_low, c_high, c_low
    bt_high, bt_low = split(b_rows.T)
    ct_high, ct_low = split(c_rows.T)
    bc[4], bc[5], bc[6], bc[7] = bt_high, bt_low, ct_high, ct_low

    def local_state(j, carry):
        part = act[j] * w_out_x[j]
        weighted[j] = part
        msg_f[j, HEAD:MSG, :] = product((bc[4], bc[5]), split(part))
        return carry

    theirs = (1 - core) * CHIPS
    mine = core * CHIPS

    def within(j, carry):
        x_pair = split(act[j])
        parts = []
        for half in range(2):
            h = 2 * j + half
            mixed = scores[...] * decay[h] * row_of(STEP, h)
            mix[h] = mixed
            parts.append(product(split(mixed), x_pair))
        inner[j] = jnp.where(first_half, parts[0], parts[1])
        return carry

    def scan(buffers, base, reverse, fill, work, result):
        msg, near, chip, row, zin, zout, zfar, back, own, other = buffers
        is_first = core == (1 if reverse else 0)
        rank = 3 - zpos if reverse else zpos

        def ranked(place):
            return (chip_at(3 - place if reverse else place, xpos), tp)

        up = ranked(jnp.minimum(rank + 1, 3))
        far = ranked(jnp.where(rank == 0, 3, 2))
        one = jnp.ones((1, ROWS), F32)
        zero = jnp.zeros((1, ROWS), F32)

        @pl.when(rank == 0)
        def _():
            zin[...] = jnp.zeros((MSG, ROWS), F32)

        @pl.when(rank <= 1)
        def _():
            zfar[...] = jnp.zeros((ROWS, ROWS), F32)

        near_copies = []
        for q in range(CHIPS):
            fill(theirs + q, 0)
            near_copies.append(copy(msg.at[theirs + q], near.at[q], base + q, (partner, tp)))
            near_copies[-1].start()
        lax.fori_loop(mine, mine + CHIPS, fill, 0)
        for q in range(CHIPS):
            near_copies[q].wait_recv()
            my_pass = msg[mine + q, 0:1, :]
            their_pass = near[q, 0:1, :]
            my_scale = jnp.where(is_first, their_pass, 1.0)
            their_scale = jnp.where(is_first, 1.0, my_pass)
            chip[q, HEAD:MSG, :] = (
                msg[mine + q, HEAD:MSG, :] * my_scale + near[q, HEAD:MSG, :] * their_scale
            )
            chip[q, 0:HEAD, :] = jnp.broadcast_to(my_pass * their_pass, (HEAD, ROWS))

        def place(k):
            return slice(0 if k == 0 else HEAD + k * PIECE, HEAD + (k + 1) * PIECE)

        def piece(k):
            return slice(k * PIECE, (k + 1) * PIECE)

        def body(k):
            return slice(HEAD + k * PIECE, HEAD + (k + 1) * PIECE)

        across = []
        for k in range(CHUNKS):
            sem = base + CHIPS + k * 3
            for step in range(1, CHIPS):
                there = lax.rem(xpos + step, CHIPS)
                across.append(
                    copy(
                        chip.at[there, place(k)],
                        row.at[xpos, place(k)],
                        sem + step - 1,
                        (chip_at(zpos, there), tp),
                    )
                )
                across[-1].start()
        row[xpos] = chip[xpos]
        lax.fori_loop(0, SOON, work, 0)
        order = list(range(CHIPS))
        if reverse:
            order = order[::-1]
        early = SOON + jnp.where(rank == 0, 0, EARLY)
        chain = base + CHIPS + 3 * CHUNKS
        around = chain + CHUNKS
        home = around + CHUNKS

        def step_up(k):
            return copy(zout.at[place(k)], zin.at[place(k)], chain + k, up)

        def step_far(k, src):
            return copy(src, zfar.at[piece(k)], around + k, far)

        held = []
        returned = []
        for k in range(CHUNKS):
            for each in across[3 * k : 3 * k + 3]:
                each.wait_recv()
            if k == 0:
                passes = [row[x, 0:1, :] for x in order]
                scales = [one]
                for x_pass in passes:
                    scales.append(scales[-1] * x_pass)
            running = row[order[0], body(k), :]
            entering = [None]
            for x, x_pass in zip(order[1:], passes[1:]):
                entering.append(running)
                running = running * x_pass + row[x, body(k), :]
            held.append(entering)
            zout[body(k), :] = running
            if k == 0:
                zout[0:HEAD, :] = jnp.broadcast_to(scales[CHIPS], (HEAD, ROWS))

            @pl.when(rank == 2)
            def _():
                step_up(k).wait_recv()
                if k == 0:
                    zout[0:HEAD, :] = zout[0:HEAD, :] * zin[0:HEAD, :]
                zout[body(k), :] = zout[body(k), :] + zin[body(k), :] * scales[CHIPS]

            @pl.when(rank <= 2)
            def _():
                step_up(k).start()

            @pl.when(rank == 0)
            def _():
                step_far(k, zout.at[body(k)]).start()

            @pl.when(rank == 3)
            def _():
                step_far(k, zfar.at[piece(k)]).wait_recv()
                step_far(k, zfar.at[piece(k)]).start()

        lax.fori_loop(SOON, early, work, 0)
        for k in range(CHUNKS):

            @pl.when(rank == 2)
            def _():
                step_far(k, zfar.at[piece(k)]).wait_recv()

            @pl.when((rank == 1) | (rank == 3))
            def _():
                step_up(k).wait_recv()

            from_before = zin[body(k), :] + zfar[piece(k), :] * zin[0:1, :]
            for x, reached, scale in zip(order, held[k], scales):
                back[x, piece(k), :] = (
                    from_before if reached is None else reached + from_before * scale
                )
            for step in range(1, CHIPS):
                there = lax.rem(xpos + step, CHIPS)
                returned.append(
                    copy(
                        back.at[there, piece(k)],
                        own.at[xpos, piece(k)],
                        home + k * 3 + step - 1,
                        (chip_at(zpos, there), tp),
                    )
                )
                returned[-1].start()
        own[xpos] = back[xpos]
        lax.fori_loop(early, PAIRS, work, 0)
        last = []
        for k in range(CHUNKS):
            for each in returned[3 * k : 3 * k + 3]:
                each.wait_recv()
            for q in range(CHIPS):
                my_pass = msg[mine + q, 0:1, :]
                their_pass = near[q, 0:1, :]
                coming = own[q, piece(k), :]
                other[q, piece(k), :] = coming * jnp.where(is_first, my_pass, one) + msg[
                    mine + q, body(k), :
                ] * jnp.where(is_first, one, zero)
                result[mine + q, piece(k), :] = coming * jnp.where(
                    is_first, one, their_pass
                ) + near[q, body(k), :] * jnp.where(is_first, zero, one)
            last.append(
                copy(
                    other.at[:, piece(k)],
                    result.at[pl.ds(mine, CHIPS), piece(k)],
                    home + 3 * CHUNKS + k,
                    (partner, tp),
                )
            )
            last[-1].start()
        for each in last:
            each.wait_recv()

        def drain():
            for each in near_copies + across + returned + last:
                each.wait_send()

            @pl.when(rank <= 2)
            def _():
                for k in range(CHUNKS):
                    step_up(k).wait_send()

            @pl.when((rank == 0) | (rank == 3))
            def _():
                for k in range(CHUNKS):
                    step_far(k, zfar.at[piece(k)]).wait_send()

        return drain

    def fill_forward(j, carry):
        return local_state(j, carry)

    scores[...] = product((c_high, c_low), (b_high, b_low), (1, 1))
    forward = (msg_f, near_f, chip_f, row_f, zin_f, zout_f, zfar_f, back_f, own_f, other_f)
    drain_forward = scan(forward, 9, False, fill_forward, within, carried)

    sums[...] = jnp.zeros((4, ROWS, ROWS), F32)

    def outputs(j, carry):
        part = product((bc[2], bc[3]), split(carried[j])) * w_in_x[j]
        read[j] = part
        total = inner[j] + part
        inner[j] = total
        gated = total * gate_act[j]
        gained = gated * norm_gain[:, lanes(j)]
        target = reference_out[:, lanes(j)].astype(F32)
        sums[0] = sums[0] + gated * gated
        sums[1] = sums[1] + gained * target
        sums[2] = sums[2] + gained * gained
        sums[3] = sums[3] + target * target
        return carry

    lax.fori_loop(0, PAIRS, outputs, 0)
    square = jnp.sum(sums[0].T, axis=0, keepdims=True) / GROUP_WIDTH + 1e-05
    dot_here = jnp.sum(sums[1].T, axis=0, keepdims=True)
    self_here = jnp.sum(sums[2].T, axis=0, keepdims=True)
    ref_here = jnp.sum(sums[3].T, axis=0, keepdims=True)
    inverse = lax.rsqrt(square)
    inverse = inverse * (1.5 - 0.5 * square * inverse * inverse)
    totals[tp] = jnp.concatenate(
        [
            dot_here * inverse,
            self_here * inverse * inverse,
            ref_here,
            jnp.zeros((5, ROWS), F32),
        ],
        axis=0,
    )
    tp_copies = []
    for step in range(1, NTP):
        there = lax.rem(tp + step, NTP)
        tp_copies.append(copy(totals.at[tp], totals.at[tp], 1 + step, (ctx, there)))
        tp_copies[-1].start()
    for each in tp_copies:
        each.wait_recv()
    total = totals[0]
    for k in range(1, NTP):
        total = total + totals[k]
    mean_all = total / D_INNER
    mean_dot, mean_self, mean_ref = mean_all[0:1], mean_all[1:2], mean_all[2:3]
    norm_self = jnp.sqrt(mean_self + 1e-06)
    norm_ref = jnp.sqrt(mean_ref + 1e-06)
    cosine = mean_dot / (norm_self * norm_ref)
    distance = jnp.sqrt(mean_self - 2.0 * mean_dot + mean_ref + 1e-06)
    lane_row = lax.broadcasted_iota(jnp.int32, (1, ROWS), 1)
    harmful = jnp.where(lane_row < LBLK, labels[0], labels[1]).astype(F32)
    coef_self = -harmful * cosine / (norm_self * norm_self) + (1.0 - harmful) / distance
    coef_ref = harmful / (norm_self * norm_ref) - (1.0 - harmful) / distance
    mean_scaled = (coef_self * inverse * self_here + coef_ref * dot_here) / GROUP_WIDTH
    sums[0] = tall(coef_self * inverse * inverse).T
    sums[1] = tall(mean_scaled * inverse * inverse * inverse).T
    sums[2] = tall(coef_ref * inverse).T

    def fill_backward(j, carry):
        gain = norm_gain[:, lanes(j)]
        target = reference_out[:, lanes(j)].astype(F32)
        mixer_out = inner[j]
        gate = gate_act[j]
        gated = mixer_out * gate
        flow = gated * (sums[0] * (gain * gain) - sums[1]) + sums[2] * (gain * target)
        out_gate[:, lanes(j)] = (flow * mixer_out * gate_slope[j]).astype(BF16)
        into = flow * gate
        grad_y[j] = into
        entering = into * w_in_x[j]
        grad_in[j] = entering
        msg_b[j, HEAD:MSG, :] = product((bc[6], bc[7]), split(entering))
        return carry

    grad_scores[...] = jnp.zeros((ROWS, ROWS), F32)
    grad_b[...] = jnp.zeros((ROWS, ROWS), F32)
    grad_c[...] = jnp.zeros((ROWS, ROWS), F32)

    def halves(value):
        turned = value.T
        return (
            jnp.sum(turned[0:64], axis=0, keepdims=True),
            jnp.sum(turned[64:128], axis=0, keepdims=True),
        )

    def within_back(j, carry):
        x_pair = split(act[j])
        flow = grad_y[j]
        flow_pair = split(flow)
        by_read = halves(read[j] * flow)
        parts = []
        for half in range(2):
            h = 2 * j + half
            picked = first_half if half == 0 else jnp.logical_not(first_half)
            only = split(jnp.where(picked, flow, 0.0))
            via = product(only, x_pair, (1, 1)) * decay[h]
            step_row = row_of(STEP, h)
            grad_scores[...] = grad_scores[...] + via * step_row
            scored = via * scores[...]
            by_step = jnp.sum(scored, axis=0, keepdims=True)
            table[GSTEP, pl.ds(h, 1), :] = by_step
            across = jnp.sum((scored * step_row).T, axis=0, keepdims=True)
            table[CUM, pl.ds(h, 1), :] = across - by_step * step_row + by_read[half]
            parts.append(product(split(mix[h].T), flow_pair))
        grad_x[j] = jnp.where(first_half, parts[0], parts[1])
        grad_c[...] = grad_c[...] + product(split(grad_in[j]), split(carried[j]), (1, 1))
        return carry

    backward = (msg_b, near_b, chip_b, row_b, zin_b, zout_b, zfar_b, back_b, own_b, other_b)
    drain_backward = scan(backward, 9 + SCAN_SEMS, True, fill_backward, within_back, adjoint)

    def finish(j, carry):
        coming = adjoint[j]
        coming_pair = split(coming)
        later = product((bc[0], bc[1]), coming_pair)
        grad = grad_x[j] + later * w_out_x[j]
        grad_pre[j, 0:ROWS, :] = grad * slope[j]
        rim_out[j] = grad_pre[j, 0:8, :]
        by_weight = halves(later * act[j])
        table[GWEIGHT, pl.ds(2 * j, 1), :] = by_weight[0]
        table[GWEIGHT, pl.ds(2 * j + 1, 1), :] = by_weight[1]
        ended = jnp.sum(carried[j] * coming, axis=0, keepdims=True)
        table[GEND, pl.ds(2 * j, 1), :] = jnp.where(lane_row < 64, ended, 0.0)
        table[GEND, pl.ds(2 * j + 1, 1), :] = jnp.where(lane_row < 64, 0.0, ended)
        grad_b[...] = grad_b[...] + product(split(weighted[j]), coming_pair, (1, 1))
        return carry

    lax.fori_loop(0, PAIRS, finish, 0)
    via_scores = grad_scores[...]
    by_b = grad_b[...] + product(split(via_scores.T), (bc[2], bc[3]))
    by_c = grad_c[...] + product(split(via_scores), (bc[0], bc[1]))
    grad_pre[PAIRS, 0:ROWS, :] = by_b * slope[PAIRS]
    grad_pre[PAIRS + 1, 0:ROWS, :] = by_c * slope[PAIRS + 1]
    rim_out[PAIRS] = grad_pre[PAIRS, 0:8, :]
    rim_out[PAIRS + 1] = grad_pre[PAIRS + 1, 0:8, :]
    rim_back = copy(rim_out, rim_in, 1, (before, tp))
    rim_back.start()
    grad_weight = table[GWEIGHT]
    leaving = grad_weight * table[WOUT]
    at_end = jnp.sum(leaving, axis=1, keepdims=True) + jnp.sum(
        table[GEND] * table[PASS], axis=1, keepdims=True
    )
    lane_16 = lax.broadcasted_iota(jnp.int32, (16, ROWS), 1)
    grad_cum = table[CUM] - leaving + jnp.where(lane_16 == ROWS - 1, at_end, 0.0)
    ones_lower = jnp.where(row_index >= lane_index, 1.0, 0.0).astype(BF16)
    grad_log = summed_by(grad_cum, ones_lower)
    grad_step = grad_weight * table[ENDS] + table[GSTEP]
    shifted_again = dt_raw[...] + down(dt_bias[...])
    rate_again = jnp.exp(down(a_log[...]))
    out_dt[...] = (grad_step - rate_again * grad_log) * sigmoid(shifted_again)

    drain_forward()
    rim_copy.wait_send()
    for each in tp_copies:
        each.wait_send()
    rim_back.wait_recv()
    inside = jnp.where(ctx == NCTX - 1, 0.0, 1.0)

    def spread_taps(i, carry):
        grad_pre[i, ROWS:MSG, :] = rim_in[i] * inside
        total = conv_weight[TAPS - 1 : TAPS, lanes(i)] * grad_pre[i, 0:ROWS, :]
        for o in range(1, TAPS):
            tap = conv_weight[TAPS - 1 - o : TAPS - o, lanes(i)]
            total = total + tap * grad_pre[i, o : ROWS + o, :] * same_after[o - 1]
        out_input[:, lanes(i)] = total.astype(BF16)
        return carry

    lax.fori_loop(0, TILES, spread_taps, 0)
    drain_backward()
    rim_back.wait_send()


def on_device(
    conv_input,
    gate_input,
    dt_raw,
    conv_weight,
    conv_bias,
    dt_bias,
    a_log,
    norm_gain,
    reference_out,
    labels,
    doc_lengths,
):
    square = (ROWS, ROWS)
    by_pair = pltpu.VMEM((PAIRS, *square), F32)
    by_tile = pltpu.VMEM((TILES, *square), F32)
    padded = pltpu.VMEM((TILES, MSG, ROWS), F32)
    one = pltpu.VMEM(square, F32)
    scans = [
        pltpu.VMEM((PAIRS, MSG, ROWS), F32),
        pltpu.VMEM((CHIPS, MSG, ROWS), F32),
        pltpu.VMEM((CHIPS, MSG, ROWS), F32),
        pltpu.VMEM((CHIPS, MSG, ROWS), F32),
        pltpu.VMEM((MSG, ROWS), F32),
        pltpu.VMEM((MSG, ROWS), F32),
        one,
        pltpu.VMEM((CHIPS, *square), F32),
        pltpu.VMEM((CHIPS, *square), F32),
        pltpu.VMEM((CHIPS, *square), F32),
    ]
    vmem = pl.BlockSpec(memory_space=pltpu.VMEM)
    far = pl.BlockSpec(memory_space=pltpu.HBM)
    held = [
        pltpu.SMEM((2,), jnp.int32),
        pltpu.SMEM((DOCS,), jnp.int32),
        pltpu.VMEM((ROWS, TILES * ROWS), BF16),
        pltpu.VMEM((ROWS, GROUP_WIDTH), BF16),
        pltpu.VMEM((16, ROWS), F32),
        pltpu.VMEM((TAPS, TILES * ROWS), F32),
        pltpu.VMEM((TILES * ROWS,), F32),
        pltpu.VMEM((1, 16), F32),
        pltpu.VMEM((1, 16), F32),
        pltpu.VMEM((1, GROUP_WIDTH), F32),
        pltpu.VMEM((ROWS, GROUP_WIDTH), BF16),
    ]
    scratch = [
        *held,
        pltpu.VMEM((TILES, ROWS), F32),
        pltpu.VMEM((16, TILES * ROWS), BF16),
        padded,
        by_tile,
        by_tile,
        by_pair,
        by_pair,
        by_pair,
        pltpu.VMEM((16, *square), F32),
        pltpu.VMEM((16, *square), F32),
        by_pair,
        by_pair,
        by_pair,
        by_pair,
        by_pair,
        by_pair,
        by_pair,
        by_pair,
        by_pair,
        padded,
        pltpu.VMEM((TILES, 8, ROWS), F32),
        pltpu.VMEM((TILES, 8, ROWS), F32),
        one,
        one,
        pltpu.VMEM((8, *square), BF16),
        pltpu.VMEM((2, PAIRS, *square), BF16),
        one,
        one,
        one,
        pltpu.VMEM((4, *square), F32),
        pltpu.VMEM((10, 16, ROWS), F32),
        pltpu.VMEM((NTP, 8, ROWS), F32),
        *scans,
        *scans,
        pltpu.SemaphoreType.DMA((9 + 2 * SCAN_SEMS,)),
        pltpu.SemaphoreType.DMA((9 + 2 * SCAN_SEMS,)),
        pltpu.SemaphoreType.DMA((11,)),
    ]
    return pl.pallas_call(
        kernel,
        out_shape=(
            jax.ShapeDtypeStruct(conv_input.shape, BF16),
            jax.ShapeDtypeStruct(gate_input.shape, BF16),
            jax.ShapeDtypeStruct(dt_raw.shape, F32),
        ),
        in_specs=[far] * 11,
        out_specs=(vmem, vmem, vmem),
        scratch_shapes=scratch,
        compiler_params=pltpu.CompilerParams(
            collective_id=0, has_side_effects=True, vmem_limit_bytes=48 * 1024 * 1024
        ),
    )(
        pltpu.with_memory_space_constraint(labels, pltpu.HBM),
        pltpu.with_memory_space_constraint(doc_lengths, pltpu.HBM),
        pltpu.with_memory_space_constraint(conv_input, pltpu.HBM),
        pltpu.with_memory_space_constraint(gate_input, pltpu.HBM),
        pltpu.with_memory_space_constraint(dt_raw, pltpu.HBM),
        pltpu.with_memory_space_constraint(conv_weight, pltpu.HBM),
        pltpu.with_memory_space_constraint(conv_bias, pltpu.HBM),
        pltpu.with_memory_space_constraint(dt_bias.reshape(1, -1), pltpu.HBM),
        pltpu.with_memory_space_constraint(a_log.reshape(1, -1), pltpu.HBM),
        pltpu.with_memory_space_constraint(norm_gain.reshape(1, -1), pltpu.HBM),
        pltpu.with_memory_space_constraint(reference_out, pltpu.HBM),
    )


def solution(mesh):
    in_specs = (
        P("ctx", "tp"),
        P("ctx", "tp"),
        P("tp", "ctx"),
        P(None, "tp"),
        P("tp"),
        P("tp"),
        P("tp"),
        P("tp"),
        P("ctx", "tp"),
        P("ctx"),
        P(),
    )
    out_specs = (P("ctx", "tp"), P("ctx", "tp"), P("tp", "ctx"))
    return jax.shard_map(
        on_device, mesh=mesh, in_specs=in_specs, out_specs=out_specs, check_vma=False
    )
```

```python
import functools

import jax
import jax.numpy as jnp
from jax import lax
from jax.experimental import pallas as pl
from jax.experimental.pallas import tpu as pltpu
from jax.sharding import PartitionSpec as P

HEADS = 128
HEAD_DIM = 64
STATE = 128
GROUPS = 8
TAPS = 4
LBLK = 64
DOCS = 8
D_INNER = 8192
GROUP_WIDTH = 1024
ROWS = 128
PAIRS = 8
TILES = 10
MSG = 136
HEAD = 8
CHUNKS = 4
PIECE = ROWS // CHUNKS
SOON = 4
EARLY = 4
CHIPS = 4
SCAN_SEMS = CHIPS + 9 * CHUNKS
NCTX = 32
NTP = 8
MESH = pl.DeviceIdType.MESH
F32 = jnp.float32
BF16 = jnp.bfloat16


def split(value):
    high = value.astype(BF16)
    return high, (value - high.astype(F32)).astype(BF16)


def one_pass(left, right, dims):
    return lax.dot_general(
        left, right, (((dims[0],), (dims[1],)), ((), ())), preferred_element_type=F32
    )


def product(left, right, dims=(1, 0)):
    left_high, left_low = left
    right_high, right_low = right
    return one_pass(left_high, right_high, dims) + (
        one_pass(left_high, right_low, dims) + one_pass(left_low, right_high, dims)
    )


def summed_by(value, ones):
    high = value.astype(BF16)
    rest = value - high.astype(F32)
    middle = rest.astype(BF16)
    low = (rest - middle.astype(F32)).astype(BF16)
    return one_pass(high, ones, (1, 0)) + (
        one_pass(middle, ones, (1, 0)) + one_pass(low, ones, (1, 0))
    )


def sigmoid(value):
    return 1.0 / (1.0 + jnp.exp(-value))


def tall(row):
    return jnp.broadcast_to(row, (ROWS, ROWS))


def two_heads(first, second):
    stacked = jnp.concatenate(
        [jnp.broadcast_to(first, (64, ROWS)), jnp.broadcast_to(second, (64, ROWS))], axis=0
    )
    return stacked.T


def kernel(
    labels_hbm,
    doc_lengths_hbm,
    conv_input_hbm,
    gate_input_hbm,
    dt_raw_hbm,
    conv_weight_hbm,
    conv_bias_hbm,
    dt_bias_hbm,
    a_log_hbm,
    norm_gain_hbm,
    reference_out_hbm,
    out_input,
    out_gate,
    out_dt,
    labels,
    doc_lengths,
    conv_input,
    gate_input,
    dt_raw,
    conv_weight,
    conv_bias,
    dt_bias,
    a_log,
    norm_gain,
    reference_out,
    bias,
    rim,
    ext,
    act,
    slope,
    w_out_x,
    w_in_x,
    weighted,
    decay,
    mix,
    inner,
    read,
    gate_act,
    gate_slope,
    grad_y,
    grad_in,
    carried,
    adjoint,
    grad_x,
    grad_pre,
    rim_out,
    rim_in,
    scores,
    mask,
    bc,
    arriving,
    grad_scores,
    grad_b,
    grad_c,
    sums,
    table,
    totals,
    msg_f,
    near_f,
    chip_f,
    row_f,
    zin_f,
    zout_f,
    zfar_f,
    back_f,
    own_f,
    other_f,
    msg_b,
    near_b,
    chip_b,
    row_b,
    zin_b,
    zout_b,
    zfar_b,
    back_b,
    own_b,
    other_b,
    send_sem,
    recv_sem,
    load_sem,
):
    ctx = lax.axis_index("ctx")
    tp = lax.axis_index("tp")
    core = lax.rem(ctx, 2)
    xpos = lax.rem(ctx // 2, CHIPS)
    zpos = ctx // (2 * CHIPS)
    partner = ctx + 1 - 2 * core
    after = lax.rem(ctx + 1, NCTX)
    before = lax.rem(ctx + NCTX - 1, NCTX)

    def chip_at(z, x):
        return (z * CHIPS + x) * 2 + core

    barrier = pltpu.get_barrier_semaphore()
    peers = [(partner, tp), (after, tp), (before, tp)]
    for step in range(1, CHIPS):
        peers.append((chip_at(zpos, lax.rem(xpos + step, CHIPS)), tp))
    peers.append((chip_at(lax.rem(zpos + 1, 4), xpos), tp))
    peers.append((chip_at(lax.rem(zpos + 3, 4), xpos), tp))
    for step in range(1, NTP):
        peers.append((ctx, lax.rem(tp + step, NTP)))
    for peer in peers:
        pl.semaphore_signal(barrier, inc=1, device_id=peer, device_id_type=MESH)

    loads = {}
    for place, (name, src, dst) in enumerate(
        (
            ("labels", labels_hbm, labels),
            ("doc_lengths", doc_lengths_hbm, doc_lengths),
            ("conv_input", conv_input_hbm, conv_input),
            ("gate_input", gate_input_hbm, gate_input),
            ("dt_raw", dt_raw_hbm, dt_raw),
            ("conv_weight", conv_weight_hbm, conv_weight),
            ("conv_bias", conv_bias_hbm, conv_bias),
            ("dt_bias", dt_bias_hbm, dt_bias),
            ("a_log", a_log_hbm, a_log),
            ("norm_gain", norm_gain_hbm, norm_gain),
            ("reference_out", reference_out_hbm, reference_out),
        )
    ):
        loads[name] = pltpu.make_async_copy(src, dst, load_sem.at[place])
        loads[name].start()

    def arrived(*which):
        for name in which:
            loads[name].wait()

    def copy(src, dst, sem, peer):
        return pltpu.make_async_remote_copy(
            src_ref=src,
            dst_ref=dst,
            send_sem=send_sem.at[sem],
            recv_sem=recv_sem.at[sem],
            device_id=peer,
            device_id_type=MESH,
        )

    row_index = lax.broadcasted_iota(jnp.int32, (ROWS, ROWS), 0)
    lane_index = lax.broadcasted_iota(jnp.int32, (ROWS, ROWS), 1)
    first_half = lane_index < 64
    first_pos = ctx * ROWS
    arrived("doc_lengths", "labels", "dt_raw", "dt_bias", "a_log")
    starts = []
    so_far = jnp.int32(0)
    for d in range(DOCS):
        starts.append(so_far)
        so_far = so_far + doc_lengths[d]

    def doc_of(position):
        found = jnp.full_like(position, -1)
        for start in starts:
            found = found + jnp.where(start <= position, 1, 0)
        return found

    docs_down = doc_of(first_pos + row_index)
    docs_across = doc_of(first_pos + lane_index)
    docs_row = docs_across[0:1, :]
    prev_doc = doc_of(jnp.full((1, ROWS), first_pos - 1, jnp.int32))
    last_doc = doc_of(jnp.full((1, ROWS), first_pos + ROWS - 1, jnp.int32))
    mask[...] = jnp.where((row_index >= lane_index) & (docs_down == docs_across), 1.0, 0.0)
    keep_out = jnp.where(docs_row == last_doc, 1.0, 0.0)
    keep_in = jnp.where(docs_row == prev_doc, 1.0, 0.0)
    through = jnp.where(prev_doc == last_doc, 1.0, 0.0)

    eye = (
        lax.broadcasted_iota(jnp.int32, (16, 16), 0) == lax.broadcasted_iota(jnp.int32, (16, 16), 1)
    )

    def down(row):
        return jnp.sum(jnp.where(eye, jnp.broadcast_to(row, (16, 16)), 0.0), axis=1, keepdims=True)

    shifted = dt_raw[...] + down(dt_bias[...])
    rate = jnp.exp(down(a_log[...]))
    small = jnp.exp(-jnp.abs(shifted))
    step_size = jnp.maximum(shifted, 0.0) + jnp.log1p(small)
    ones_upper = jnp.where(row_index <= lane_index, 1.0, 0.0).astype(BF16)
    log_cumul = summed_by(-rate * step_size, ones_upper)
    log_end = log_cumul[:, ROWS - 1 : ROWS]
    ends = jnp.exp(log_end - log_cumul) * keep_out
    w_out = ends * step_size
    w_in = jnp.exp(log_cumul) * keep_in
    passing = jnp.broadcast_to(jnp.exp(log_end), (16, ROWS)) * through
    LOG, STEP, ENDS, WOUT, WIN, PASS, CUM, GSTEP, GWEIGHT, GEND = range(10)
    table[LOG] = log_cumul
    table[STEP] = step_size
    table[ENDS] = ends
    table[WOUT] = w_out
    table[WIN] = w_in
    table[PASS] = passing

    arrived("conv_input")
    pl.semaphore_wait(barrier, len(peers))
    rim_copy = copy(conv_input.at[ROWS - 16 : ROWS], rim, 0, (after, tp))
    rim_copy.start()

    def lanes(i):
        return pl.ds(pl.multiple_of(i * ROWS, ROWS), ROWS)

    def row_of(which, h):
        return table[which, pl.ds(h, 1), :]

    def expand(j, carry):
        w_out_x[j] = two_heads(row_of(WOUT, 2 * j), row_of(WOUT, 2 * j + 1))
        w_in_x[j] = two_heads(row_of(WIN, 2 * j), row_of(WIN, 2 * j + 1))
        lane_row = lax.broadcasted_iota(jnp.int32, (1, ROWS), 1)
        pass_row = jnp.where(lane_row < 64, row_of(PASS, 2 * j), row_of(PASS, 2 * j + 1))
        pass_rows = jnp.broadcast_to(pass_row, (8, ROWS))
        msg_f[j, 0:HEAD, :] = pass_rows
        msg_b[j, 0:HEAD, :] = pass_rows
        return carry

    lax.fori_loop(0, PAIRS, expand, 0, unroll=8)

    same_before = [
        jnp.where(doc_of(first_pos + row_index - o) == docs_down, 1.0, 0.0) for o in range(1, TAPS)
    ]
    same_after = [
        jnp.where(doc_of(first_pos + row_index + o) == docs_down, 1.0, 0.0) for o in range(1, TAPS)
    ]

    arrived("conv_bias", "conv_weight")
    for i in range(TILES):
        bias[i : i + 1, :] = conv_bias[i * ROWS : (i + 1) * ROWS].reshape(1, ROWS)

    def convolve(i, carry):
        ext[i, 8:MSG, :] = conv_input[:, lanes(i)].astype(F32)
        ext[i, 0:8, :] = jnp.zeros((8, ROWS), F32)
        pre = bias[pl.ds(i, 1), :] + conv_weight[TAPS - 1 : TAPS, lanes(i)] * ext[i, 8:MSG, :]
        for o in range(1, TAPS):
            tap = conv_weight[TAPS - 1 - o : TAPS - o, lanes(i)]
            pre = pre + tap * ext[i, 8 - o : MSG - o, :] * same_before[o - 1]
        sigma = sigmoid(pre)
        act[i] = pre * sigma
        slope[i] = sigma * (1.0 + pre * (1.0 - sigma))
        return carry

    lax.fori_loop(0, TILES, convolve, 0, unroll=10)

    arrived("gate_input", "reference_out", "norm_gain")

    def gates(j, carry):
        gate = gate_input[:, lanes(j)].astype(F32)
        sigma = sigmoid(gate)
        gate_act[j] = gate * sigma
        gate_slope[j] = sigma * (1.0 + gate * (1.0 - sigma))
        for half in range(2):
            across = tall(row_of(LOG, 2 * j + half))
            gap = across.T - across
            decay[2 * j + half] = jnp.exp(jnp.where(mask[...] > 0.0, gap, -1e30))
        return carry

    lax.fori_loop(0, PAIRS, gates, 0, unroll=8)
    rim_copy.wait_recv()

    def convolve_top(i, carry):
        ext[i, 0:8, :] = rim[:, lanes(i)].astype(F32)[8:16]
        pre = bias[pl.ds(i, 1), :] + conv_weight[TAPS - 1 : TAPS, lanes(i)] * ext[i, 8:16, :]
        for o in range(1, TAPS):
            tap = conv_weight[TAPS - 1 - o : TAPS - o, lanes(i)]
            pre = pre + tap * ext[i, 8 - o : 16 - o, :] * same_before[o - 1][0:8]
        sigma = sigmoid(pre)
        act[i, 0:8, :] = pre * sigma
        slope[i, 0:8, :] = sigma * (1.0 + pre * (1.0 - sigma))
        return carry

    lax.fori_loop(0, TILES, convolve_top, 0, unroll=10)

    b_rows = act[PAIRS]
    c_rows = act[PAIRS + 1]
    b_high, b_low = split(b_rows)
    c_high, c_low = split(c_rows)
    bc[0], bc[1], bc[2], bc[3] = b_high, b_low, c_high, c_low
    bt_high, bt_low = split(b_rows.T)
    ct_high, ct_low = split(c_rows.T)
    bc[4], bc[5], bc[6], bc[7] = bt_high, bt_low, ct_high, ct_low

    def local_state(j, carry):
        part = act[j] * w_out_x[j]
        weighted[j] = part
        msg_f[j, HEAD:MSG, :] = product((bc[4], bc[5]), split(part))
        return carry

    theirs = (1 - core) * CHIPS
    mine = core * CHIPS

    def within(j, carry):
        x_pair = split(act[j])
        parts = []
        for half in range(2):
            h = 2 * j + half
            mixed = scores[...] * decay[h] * row_of(STEP, h)
            mix[h] = mixed
            parts.append(product(split(mixed), x_pair))
        inner[j] = jnp.where(first_half, parts[0], parts[1])
        return carry

    def scan(buffers, base, reverse, fill, work, result):
        msg, near, chip, row, zin, zout, zfar, back, own, other = buffers
        is_first = core == (1 if reverse else 0)
        rank = 3 - zpos if reverse else zpos

        def ranked(place):
            return (chip_at(3 - place if reverse else place, xpos), tp)

        up = ranked(jnp.minimum(rank + 1, 3))
        far = ranked(jnp.where(rank == 0, 3, 2))
        one = jnp.ones((1, ROWS), F32)
        zero = jnp.zeros((1, ROWS), F32)

        @pl.when(rank == 0)
        def _():
            zin[...] = jnp.zeros((MSG, ROWS), F32)

        @pl.when(rank <= 1)
        def _():
            zfar[...] = jnp.zeros((ROWS, ROWS), F32)

        near_copies = []
        for q in range(CHIPS):
            fill(theirs + q, 0)
            near_copies.append(copy(msg.at[theirs + q], near.at[q], base + q, (partner, tp)))
            near_copies[-1].start()
        for q in range(CHIPS):
            fill(mine + q, 0)
        for q in range(CHIPS):
            near_copies[q].wait_recv()
            my_pass = msg[mine + q, 0:1, :]
            their_pass = near[q, 0:1, :]
            my_scale = jnp.where(is_first, their_pass, 1.0)
            their_scale = jnp.where(is_first, 1.0, my_pass)
            chip[q, HEAD:MSG, :] = (
                msg[mine + q, HEAD:MSG, :] * my_scale + near[q, HEAD:MSG, :] * their_scale
            )
            chip[q, 0:HEAD, :] = jnp.broadcast_to(my_pass * their_pass, (HEAD, ROWS))

        def place(k):
            return slice(0 if k == 0 else HEAD + k * PIECE, HEAD + (k + 1) * PIECE)

        def piece(k):
            return slice(k * PIECE, (k + 1) * PIECE)

        def body(k):
            return slice(HEAD + k * PIECE, HEAD + (k + 1) * PIECE)

        across = []
        for k in range(CHUNKS):
            sem = base + CHIPS + k * 3
            for step in (2, 1, 3):
                there = lax.rem(xpos + step, CHIPS)
                across.append(
                    copy(
                        chip.at[there, place(k)],
                        row.at[xpos, place(k)],
                        sem + step - 1,
                        (chip_at(zpos, there), tp),
                    )
                )
                across[-1].start()
        row[xpos] = chip[xpos]
        lax.fori_loop(0, SOON, work, 0)
        order = list(range(CHIPS))
        if reverse:
            order = order[::-1]
        early = SOON + jnp.where(rank == 0, 0, EARLY)
        chain = base + CHIPS + 3 * CHUNKS
        around = chain + CHUNKS
        home = around + CHUNKS

        def step_up(k):
            return copy(zout.at[place(k)], zin.at[place(k)], chain + k, up)

        def step_far(k, src):
            return copy(src, zfar.at[piece(k)], around + k, far)

        held = []
        returned = []
        for k in range(CHUNKS):
            for each in across[3 * k : 3 * k + 3]:
                each.wait_recv()
            if k == 0:
                passes = [row[x, 0:1, :] for x in order]
                scales = [one]
                for x_pass in passes:
                    scales.append(scales[-1] * x_pass)
            running = row[order[0], body(k), :]
            entering = [None]
            for x, x_pass in zip(order[1:], passes[1:]):
                entering.append(running)
                running = running * x_pass + row[x, body(k), :]
            held.append(entering)
            zout[body(k), :] = running
            if k == 0:
                zout[0:HEAD, :] = jnp.broadcast_to(scales[CHIPS], (HEAD, ROWS))

            @pl.when(rank == 2)
            def _():
                step_up(k).wait_recv()
                if k == 0:
                    zout[0:HEAD, :] = zout[0:HEAD, :] * zin[0:HEAD, :]
                zout[body(k), :] = zout[body(k), :] + zin[body(k), :] * scales[CHIPS]

            @pl.when(rank <= 2)
            def _():
                step_up(k).start()

            @pl.when(rank == 0)
            def _():
                step_far(k, zout.at[body(k)]).start()

            @pl.when(rank == 3)
            def _():
                step_far(k, zfar.at[piece(k)]).wait_recv()
                step_far(k, zfar.at[piece(k)]).start()

        lax.fori_loop(SOON, early, work, 0)
        for k in range(CHUNKS):

            @pl.when(rank == 2)
            def _():
                step_far(k, zfar.at[piece(k)]).wait_recv()

            @pl.when((rank == 1) | (rank == 3))
            def _():
                step_up(k).wait_recv()

            from_before = zin[body(k), :] + zfar[piece(k), :] * zin[0:1, :]
            for x, reached, scale in zip(order, held[k], scales):
                back[x, piece(k), :] = (
                    from_before if reached is None else reached + from_before * scale
                )
            for step in (2, 1, 3):
                there = lax.rem(xpos + step, CHIPS)
                returned.append(
                    copy(
                        back.at[there, piece(k)],
                        own.at[xpos, piece(k)],
                        home + k * 3 + step - 1,
                        (chip_at(zpos, there), tp),
                    )
                )
                returned[-1].start()
        own[xpos] = back[xpos]
        lax.fori_loop(early, PAIRS, work, 0)
        last = []
        for k in range(CHUNKS):
            for each in returned[3 * k : 3 * k + 3]:
                each.wait_recv()
            for q in range(CHIPS):
                my_pass = msg[mine + q, 0:1, :]
                their_pass = near[q, 0:1, :]
                coming = own[q, piece(k), :]
                other[q, piece(k), :] = coming * jnp.where(is_first, my_pass, one) + msg[
                    mine + q, body(k), :
                ] * jnp.where(is_first, one, zero)
                result[mine + q, piece(k), :] = coming * jnp.where(
                    is_first, one, their_pass
                ) + near[q, body(k), :] * jnp.where(is_first, zero, one)
            last.append(
                copy(
                    other.at[:, piece(k)],
                    result.at[pl.ds(mine, CHIPS), piece(k)],
                    home + 3 * CHUNKS + k,
                    (partner, tp),
                )
            )
            last[-1].start()
        for each in last:
            each.wait_recv()

        def drain():
            for each in near_copies + across + returned + last:
                each.wait_send()

            @pl.when(rank <= 2)
            def _():
                for k in range(CHUNKS):
                    step_up(k).wait_send()

            @pl.when((rank == 0) | (rank == 3))
            def _():
                for k in range(CHUNKS):
                    step_far(k, zfar.at[piece(k)]).wait_send()

        return drain

    def fill_forward(j, carry):
        return local_state(j, carry)

    scores[...] = product((c_high, c_low), (b_high, b_low), (1, 1))
    forward = (msg_f, near_f, chip_f, row_f, zin_f, zout_f, zfar_f, back_f, own_f, other_f)
    drain_forward = scan(forward, 9, False, fill_forward, within, carried)

    sums[...] = jnp.zeros((4, ROWS, ROWS), F32)

    def outputs(j, carry):
        part = product((bc[2], bc[3]), split(carried[j])) * w_in_x[j]
        read[j] = part
        total = inner[j] + part
        inner[j] = total
        gated = total * gate_act[j]
        gained = gated * norm_gain[:, lanes(j)]
        target = reference_out[:, lanes(j)].astype(F32)
        sums[0] = sums[0] + gated * gated
        sums[1] = sums[1] + gained * target
        sums[2] = sums[2] + gained * gained
        sums[3] = sums[3] + target * target
        return carry

    lax.fori_loop(0, PAIRS, outputs, 0, unroll=8)
    square = jnp.sum(sums[0].T, axis=0, keepdims=True) / GROUP_WIDTH + 1e-05
    dot_here = jnp.sum(sums[1].T, axis=0, keepdims=True)
    self_here = jnp.sum(sums[2].T, axis=0, keepdims=True)
    ref_here = jnp.sum(sums[3].T, axis=0, keepdims=True)
    inverse = lax.rsqrt(square)
    inverse = inverse * (1.5 - 0.5 * square * inverse * inverse)
    totals[tp] = jnp.concatenate(
        [
            dot_here * inverse,
            self_here * inverse * inverse,
            ref_here,
            jnp.zeros((5, ROWS), F32),
        ],
        axis=0,
    )
    tp_copies = []
    for step in range(1, NTP):
        there = lax.rem(tp + step, NTP)
        tp_copies.append(copy(totals.at[tp], totals.at[tp], 1 + step, (ctx, there)))
        tp_copies[-1].start()
    for each in tp_copies:
        each.wait_recv()
    total = totals[0]
    for k in range(1, NTP):
        total = total + totals[k]
    mean_all = total / D_INNER
    mean_dot, mean_self, mean_ref = mean_all[0:1], mean_all[1:2], mean_all[2:3]
    norm_self = jnp.sqrt(mean_self + 1e-06)
    norm_ref = jnp.sqrt(mean_ref + 1e-06)
    cosine = mean_dot / (norm_self * norm_ref)
    distance = jnp.sqrt(mean_self - 2.0 * mean_dot + mean_ref + 1e-06)
    lane_row = lax.broadcasted_iota(jnp.int32, (1, ROWS), 1)
    harmful = jnp.where(lane_row < LBLK, labels[0], labels[1]).astype(F32)
    coef_self = -harmful * cosine / (norm_self * norm_self) + (1.0 - harmful) / distance
    coef_ref = harmful / (norm_self * norm_ref) - (1.0 - harmful) / distance
    mean_scaled = (coef_self * inverse * self_here + coef_ref * dot_here) / GROUP_WIDTH
    sums[0] = tall(coef_self * inverse * inverse).T
    sums[1] = tall(mean_scaled * inverse * inverse * inverse).T
    sums[2] = tall(coef_ref * inverse).T

    def fill_backward(j, carry):
        gain = norm_gain[:, lanes(j)]
        target = reference_out[:, lanes(j)].astype(F32)
        mixer_out = inner[j]
        gate = gate_act[j]
        gated = mixer_out * gate
        flow = gated * (sums[0] * (gain * gain) - sums[1]) + sums[2] * (gain * target)
        out_gate[:, lanes(j)] = (flow * mixer_out * gate_slope[j]).astype(BF16)
        into = flow * gate
        grad_y[j] = into
        entering = into * w_in_x[j]
        grad_in[j] = entering
        msg_b[j, HEAD:MSG, :] = product((bc[6], bc[7]), split(entering))
        return carry

    grad_scores[...] = jnp.zeros((ROWS, ROWS), F32)
    grad_b[...] = jnp.zeros((ROWS, ROWS), F32)
    grad_c[...] = jnp.zeros((ROWS, ROWS), F32)

    def halves(value):
        turned = value.T
        return (
            jnp.sum(turned[0:64], axis=0, keepdims=True),
            jnp.sum(turned[64:128], axis=0, keepdims=True),
        )

    def within_back(j, carry):
        x_pair = split(act[j])
        flow = grad_y[j]
        flow_pair = split(flow)
        by_read = halves(read[j] * flow)
        parts = []
        for half in range(2):
            h = 2 * j + half
            picked = first_half if half == 0 else jnp.logical_not(first_half)
            only = split(jnp.where(picked, flow, 0.0))
            via = product(only, x_pair, (1, 1)) * decay[h]
            step_row = row_of(STEP, h)
            grad_scores[...] = grad_scores[...] + via * step_row
            scored = via * scores[...]
            by_step = jnp.sum(scored, axis=0, keepdims=True)
            table[GSTEP, pl.ds(h, 1), :] = by_step
            across = jnp.sum((scored * step_row).T, axis=0, keepdims=True)
            table[CUM, pl.ds(h, 1), :] = across - by_step * step_row + by_read[half]
            parts.append(product(split(mix[h].T), flow_pair))
        grad_x[j] = jnp.where(first_half, parts[0], parts[1])
        grad_c[...] = grad_c[...] + product(split(grad_in[j]), split(carried[j]), (1, 1))
        return carry

    backward = (msg_b, near_b, chip_b, row_b, zin_b, zout_b, zfar_b, back_b, own_b, other_b)
    drain_backward = scan(backward, 9 + SCAN_SEMS, True, fill_backward, within_back, adjoint)

    def finish(j, carry):
        coming = adjoint[j]
        coming_pair = split(coming)
        later = product((bc[0], bc[1]), coming_pair)
        grad = grad_x[j] + later * w_out_x[j]
        grad_pre[j, 0:ROWS, :] = grad * slope[j]
        rim_out[j] = grad_pre[j, 0:8, :]
        by_weight = halves(later * act[j])
        table[GWEIGHT, pl.ds(2 * j, 1), :] = by_weight[0]
        table[GWEIGHT, pl.ds(2 * j + 1, 1), :] = by_weight[1]
        ended = jnp.sum(carried[j] * coming, axis=0, keepdims=True)
        table[GEND, pl.ds(2 * j, 1), :] = jnp.where(lane_row < 64, ended, 0.0)
        table[GEND, pl.ds(2 * j + 1, 1), :] = jnp.where(lane_row < 64, 0.0, ended)
        grad_b[...] = grad_b[...] + product(split(weighted[j]), coming_pair, (1, 1))
        return carry

    lax.fori_loop(0, PAIRS, finish, 0, unroll=8)
    via_scores = grad_scores[...]
    by_b = grad_b[...] + product(split(via_scores.T), (bc[2], bc[3]))
    by_c = grad_c[...] + product(split(via_scores), (bc[0], bc[1]))
    grad_pre[PAIRS, 0:ROWS, :] = by_b * slope[PAIRS]
    grad_pre[PAIRS + 1, 0:ROWS, :] = by_c * slope[PAIRS + 1]
    rim_out[PAIRS] = grad_pre[PAIRS, 0:8, :]
    rim_out[PAIRS + 1] = grad_pre[PAIRS + 1, 0:8, :]
    rim_back = copy(rim_out, rim_in, 1, (before, tp))
    rim_back.start()
    grad_weight = table[GWEIGHT]
    leaving = grad_weight * table[WOUT]
    at_end = jnp.sum(leaving, axis=1, keepdims=True) + jnp.sum(
        table[GEND] * table[PASS], axis=1, keepdims=True
    )
    lane_16 = lax.broadcasted_iota(jnp.int32, (16, ROWS), 1)
    grad_cum = table[CUM] - leaving + jnp.where(lane_16 == ROWS - 1, at_end, 0.0)
    ones_lower = jnp.where(row_index >= lane_index, 1.0, 0.0).astype(BF16)
    grad_log = summed_by(grad_cum, ones_lower)
    grad_step = grad_weight * table[ENDS] + table[GSTEP]
    shifted_again = dt_raw[...] + down(dt_bias[...])
    rate_again = jnp.exp(down(a_log[...]))
    out_dt[...] = (grad_step - rate_again * grad_log) * sigmoid(shifted_again)

    drain_forward()
    rim_copy.wait_send()
    for each in tp_copies:
        each.wait_send()
    rim_back.wait_recv()
    inside = jnp.where(ctx == NCTX - 1, 0.0, 1.0)

    def spread_taps(i, carry):
        grad_pre[i, ROWS:MSG, :] = rim_in[i] * inside
        total = conv_weight[TAPS - 1 : TAPS, lanes(i)] * grad_pre[i, 0:ROWS, :]
        for o in range(1, TAPS):
            tap = conv_weight[TAPS - 1 - o : TAPS - o, lanes(i)]
            total = total + tap * grad_pre[i, o : ROWS + o, :] * same_after[o - 1]
        out_input[:, lanes(i)] = total.astype(BF16)
        return carry

    lax.fori_loop(0, TILES, spread_taps, 0, unroll=10)
    drain_backward()
    rim_back.wait_send()


def on_device(
    conv_input,
    gate_input,
    dt_raw,
    conv_weight,
    conv_bias,
    dt_bias,
    a_log,
    norm_gain,
    reference_out,
    labels,
    doc_lengths,
):
    square = (ROWS, ROWS)
    by_pair = pltpu.VMEM((PAIRS, *square), F32)
    by_tile = pltpu.VMEM((TILES, *square), F32)
    padded = pltpu.VMEM((TILES, MSG, ROWS), F32)
    one = pltpu.VMEM(square, F32)
    scans = [
        pltpu.VMEM((PAIRS, MSG, ROWS), F32),
        pltpu.VMEM((CHIPS, MSG, ROWS), F32),
        pltpu.VMEM((CHIPS, MSG, ROWS), F32),
        pltpu.VMEM((CHIPS, MSG, ROWS), F32),
        pltpu.VMEM((MSG, ROWS), F32),
        pltpu.VMEM((MSG, ROWS), F32),
        one,
        pltpu.VMEM((CHIPS, *square), F32),
        pltpu.VMEM((CHIPS, *square), F32),
        pltpu.VMEM((CHIPS, *square), F32),
    ]
    vmem = pl.BlockSpec(memory_space=pltpu.VMEM)
    far = pl.BlockSpec(memory_space=pltpu.HBM)
    held = [
        pltpu.SMEM((2,), jnp.int32),
        pltpu.SMEM((DOCS,), jnp.int32),
        pltpu.VMEM((ROWS, TILES * ROWS), BF16),
        pltpu.VMEM((ROWS, GROUP_WIDTH), BF16),
        pltpu.VMEM((16, ROWS), F32),
        pltpu.VMEM((TAPS, TILES * ROWS), F32),
        pltpu.VMEM((TILES * ROWS,), F32),
        pltpu.VMEM((1, 16), F32),
        pltpu.VMEM((1, 16), F32),
        pltpu.VMEM((1, GROUP_WIDTH), F32),
        pltpu.VMEM((ROWS, GROUP_WIDTH), BF16),
    ]
    scratch = [
        *held,
        pltpu.VMEM((TILES, ROWS), F32),
        pltpu.VMEM((16, TILES * ROWS), BF16),
        padded,
        by_tile,
        by_tile,
        by_pair,
        by_pair,
        by_pair,
        pltpu.VMEM((16, *square), F32),
        pltpu.VMEM((16, *square), F32),
        by_pair,
        by_pair,
        by_pair,
        by_pair,
        by_pair,
        by_pair,
        by_pair,
        by_pair,
        by_pair,
        padded,
        pltpu.VMEM((TILES, 8, ROWS), F32),
        pltpu.VMEM((TILES, 8, ROWS), F32),
        one,
        one,
        pltpu.VMEM((8, *square), BF16),
        pltpu.VMEM((2, PAIRS, *square), BF16),
        one,
        one,
        one,
        pltpu.VMEM((4, *square), F32),
        pltpu.VMEM((10, 16, ROWS), F32),
        pltpu.VMEM((NTP, 8, ROWS), F32),
        *scans,
        *scans,
        pltpu.SemaphoreType.DMA((9 + 2 * SCAN_SEMS,)),
        pltpu.SemaphoreType.DMA((9 + 2 * SCAN_SEMS,)),
        pltpu.SemaphoreType.DMA((11,)),
    ]
    return pl.pallas_call(
        kernel,
        out_shape=(
            jax.ShapeDtypeStruct(conv_input.shape, BF16),
            jax.ShapeDtypeStruct(gate_input.shape, BF16),
            jax.ShapeDtypeStruct(dt_raw.shape, F32),
        ),
        in_specs=[far] * 11,
        out_specs=(vmem, vmem, vmem),
        scratch_shapes=scratch,
        compiler_params=pltpu.CompilerParams(
            collective_id=0, has_side_effects=True, vmem_limit_bytes=48 * 1024 * 1024
        ),
    )(
        pltpu.with_memory_space_constraint(labels, pltpu.HBM),
        pltpu.with_memory_space_constraint(doc_lengths, pltpu.HBM),
        pltpu.with_memory_space_constraint(conv_input, pltpu.HBM),
        pltpu.with_memory_space_constraint(gate_input, pltpu.HBM),
        pltpu.with_memory_space_constraint(dt_raw, pltpu.HBM),
        pltpu.with_memory_space_constraint(conv_weight, pltpu.HBM),
        pltpu.with_memory_space_constraint(conv_bias, pltpu.HBM),
        pltpu.with_memory_space_constraint(dt_bias.reshape(1, -1), pltpu.HBM),
        pltpu.with_memory_space_constraint(a_log.reshape(1, -1), pltpu.HBM),
        pltpu.with_memory_space_constraint(norm_gain.reshape(1, -1), pltpu.HBM),
        pltpu.with_memory_space_constraint(reference_out, pltpu.HBM),
    )


def solution(mesh):
    in_specs = (
        P("ctx", "tp"),
        P("ctx", "tp"),
        P("tp", "ctx"),
        P(None, "tp"),
        P("tp"),
        P("tp"),
        P("tp"),
        P("tp"),
        P("ctx", "tp"),
        P("ctx"),
        P(),
    )
    out_specs = (P("ctx", "tp"), P("ctx", "tp"), P("tp", "ctx"))
    return jax.shard_map(
        on_device, mesh=mesh, in_specs=in_specs, out_specs=out_specs, check_vma=False
    )
```

```python
import functools

import jax
import jax.numpy as jnp
from jax import lax
from jax.experimental import pallas as pl
from jax.experimental.pallas import tpu as pltpu
from jax.sharding import PartitionSpec as P

HEADS = 128
HEAD_DIM = 64
STATE = 128
GROUPS = 8
TAPS = 4
LBLK = 64
DOCS = 8
D_INNER = 8192
GROUP_WIDTH = 1024
ROWS = 128
PAIRS = 8
TILES = 10
MSG = 136
HEAD = 8
CHUNKS = 4
PIECE = ROWS // CHUNKS
SOON = 4
EARLY = 4
CHIPS = 4
SCAN_SEMS = CHIPS + 9 * CHUNKS
NCTX = 32
NTP = 8
MESH = pl.DeviceIdType.MESH
F32 = jnp.float32
BF16 = jnp.bfloat16


def split(value):
    high = value.astype(BF16)
    return high, (value - high.astype(F32)).astype(BF16)


def one_pass(left, right, dims):
    return lax.dot_general(
        left, right, (((dims[0],), (dims[1],)), ((), ())), preferred_element_type=F32
    )


def product(left, right, dims=(1, 0)):
    left_high, left_low = left
    right_high, right_low = right
    return one_pass(left_high, right_high, dims) + (
        one_pass(left_high, right_low, dims) + one_pass(left_low, right_high, dims)
    )


def summed_by(value, ones):
    high = value.astype(BF16)
    rest = value - high.astype(F32)
    middle = rest.astype(BF16)
    low = (rest - middle.astype(F32)).astype(BF16)
    return one_pass(high, ones, (1, 0)) + (
        one_pass(middle, ones, (1, 0)) + one_pass(low, ones, (1, 0))
    )


def sigmoid(value):
    return 1.0 / (1.0 + jnp.exp(-value))


def tall(row):
    return jnp.broadcast_to(row, (ROWS, ROWS))


def two_heads(first, second):
    stacked = jnp.concatenate(
        [jnp.broadcast_to(first, (64, ROWS)), jnp.broadcast_to(second, (64, ROWS))], axis=0
    )
    return stacked.T


def kernel(
    labels_hbm,
    doc_lengths_hbm,
    conv_input_hbm,
    gate_input_hbm,
    dt_raw_hbm,
    conv_weight_hbm,
    conv_bias_hbm,
    dt_bias_hbm,
    a_log_hbm,
    norm_gain_hbm,
    reference_out_hbm,
    out_input,
    out_gate,
    out_dt,
    labels,
    doc_lengths,
    conv_input,
    gate_input,
    dt_raw,
    conv_weight,
    conv_bias,
    dt_bias,
    a_log,
    norm_gain,
    reference_out,
    bias,
    rim,
    ext,
    act,
    slope,
    w_out_x,
    w_in_x,
    weighted,
    decay,
    mix,
    inner,
    read,
    gate_act,
    gate_slope,
    grad_y,
    grad_in,
    carried,
    adjoint,
    grad_x,
    grad_pre,
    rim_out,
    rim_in,
    scores,
    mask,
    bc,
    arriving,
    grad_scores,
    grad_b,
    grad_c,
    sums,
    table,
    totals,
    msg_f,
    near_f,
    chip_f,
    row_f,
    zin_f,
    zout_f,
    zfar_f,
    back_f,
    own_f,
    other_f,
    msg_b,
    near_b,
    chip_b,
    row_b,
    zin_b,
    zout_b,
    zfar_b,
    back_b,
    own_b,
    other_b,
    send_sem,
    recv_sem,
    load_sem,
):
    ctx = lax.axis_index("ctx")
    tp = lax.axis_index("tp")
    core = lax.rem(ctx, 2)
    xpos = lax.rem(ctx // 2, CHIPS)
    zpos = ctx // (2 * CHIPS)
    partner = ctx + 1 - 2 * core
    after = lax.rem(ctx + 1, NCTX)
    before = lax.rem(ctx + NCTX - 1, NCTX)

    def chip_at(z, x):
        return (z * CHIPS + x) * 2 + core

    barrier = pltpu.get_barrier_semaphore()
    peers = [(partner, tp), (after, tp), (before, tp)]
    for step in range(1, CHIPS):
        peers.append((chip_at(zpos, lax.rem(xpos + step, CHIPS)), tp))
    peers.append((chip_at(lax.rem(zpos + 1, 4), xpos), tp))
    peers.append((chip_at(lax.rem(zpos + 3, 4), xpos), tp))
    for step in range(1, NTP):
        peers.append((ctx, lax.rem(tp + step, NTP)))
    for peer in peers:
        pl.semaphore_signal(barrier, inc=1, device_id=peer, device_id_type=MESH)

    loads = {}
    for place, (name, src, dst) in enumerate(
        (
            ("labels", labels_hbm, labels),
            ("doc_lengths", doc_lengths_hbm, doc_lengths),
            ("conv_input", conv_input_hbm, conv_input),
            ("gate_input", gate_input_hbm, gate_input),
            ("dt_raw", dt_raw_hbm, dt_raw),
            ("conv_weight", conv_weight_hbm, conv_weight),
            ("conv_bias", conv_bias_hbm, conv_bias),
            ("dt_bias", dt_bias_hbm, dt_bias),
            ("a_log", a_log_hbm, a_log),
            ("norm_gain", norm_gain_hbm, norm_gain),
            ("reference_out", reference_out_hbm, reference_out),
        )
    ):
        loads[name] = pltpu.make_async_copy(src, dst, load_sem.at[place])
        loads[name].start()

    def arrived(*which):
        for name in which:
            loads[name].wait()

    def copy(src, dst, sem, peer):
        return pltpu.make_async_remote_copy(
            src_ref=src,
            dst_ref=dst,
            send_sem=send_sem.at[sem],
            recv_sem=recv_sem.at[sem],
            device_id=peer,
            device_id_type=MESH,
        )

    row_index = lax.broadcasted_iota(jnp.int32, (ROWS, ROWS), 0)
    lane_index = lax.broadcasted_iota(jnp.int32, (ROWS, ROWS), 1)
    first_half = lane_index < 64
    first_pos = ctx * ROWS
    arrived("doc_lengths", "labels", "dt_raw", "dt_bias", "a_log")
    starts = []
    so_far = jnp.int32(0)
    for d in range(DOCS):
        starts.append(so_far)
        so_far = so_far + doc_lengths[d]

    def doc_of(position):
        found = jnp.full_like(position, -1)
        for start in starts:
            found = found + jnp.where(start <= position, 1, 0)
        return found

    docs_down = doc_of(first_pos + row_index)
    docs_across = doc_of(first_pos + lane_index)
    docs_row = docs_across[0:1, :]
    prev_doc = doc_of(jnp.full((1, ROWS), first_pos - 1, jnp.int32))
    last_doc = doc_of(jnp.full((1, ROWS), first_pos + ROWS - 1, jnp.int32))
    mask[...] = jnp.where((row_index >= lane_index) & (docs_down == docs_across), 1.0, 0.0)
    keep_out = jnp.where(docs_row == last_doc, 1.0, 0.0)
    keep_in = jnp.where(docs_row == prev_doc, 1.0, 0.0)
    through = jnp.where(prev_doc == last_doc, 1.0, 0.0)

    eye = (
        lax.broadcasted_iota(jnp.int32, (16, 16), 0) == lax.broadcasted_iota(jnp.int32, (16, 16), 1)
    )

    def down(row):
        return jnp.sum(jnp.where(eye, jnp.broadcast_to(row, (16, 16)), 0.0), axis=1, keepdims=True)

    shifted = dt_raw[...] + down(dt_bias[...])
    rate = jnp.exp(down(a_log[...]))
    small = jnp.exp(-jnp.abs(shifted))
    step_size = jnp.maximum(shifted, 0.0) + jnp.log1p(small)
    ones_upper = jnp.where(row_index <= lane_index, 1.0, 0.0).astype(BF16)
    log_cumul = summed_by(-rate * step_size, ones_upper)
    log_end = log_cumul[:, ROWS - 1 : ROWS]
    ends = jnp.exp(log_end - log_cumul) * keep_out
    w_out = ends * step_size
    w_in = jnp.exp(log_cumul) * keep_in
    passing = jnp.broadcast_to(jnp.exp(log_end), (16, ROWS)) * through
    LOG, STEP, ENDS, WOUT, WIN, PASS, CUM, GSTEP, GWEIGHT, GEND = range(10)
    table[LOG] = log_cumul
    table[STEP] = step_size
    table[ENDS] = ends
    table[WOUT] = w_out
    table[WIN] = w_in
    table[PASS] = passing

    arrived("conv_input")
    pl.semaphore_wait(barrier, len(peers))
    rim_copy = copy(conv_input.at[ROWS - 16 : ROWS], rim, 0, (after, tp))
    rim_copy.start()

    def lanes(i):
        return pl.ds(pl.multiple_of(i * ROWS, ROWS), ROWS)

    def row_of(which, h):
        return table[which, pl.ds(h, 1), :]

    def expand(j, carry):
        w_out_x[j] = two_heads(row_of(WOUT, 2 * j), row_of(WOUT, 2 * j + 1))
        w_in_x[j] = two_heads(row_of(WIN, 2 * j), row_of(WIN, 2 * j + 1))
        lane_row = lax.broadcasted_iota(jnp.int32, (1, ROWS), 1)
        pass_row = jnp.where(lane_row < 64, row_of(PASS, 2 * j), row_of(PASS, 2 * j + 1))
        pass_rows = jnp.broadcast_to(pass_row, (8, ROWS))
        msg_f[j, 0:HEAD, :] = pass_rows
        msg_b[j, 0:HEAD, :] = pass_rows
        return carry

    lax.fori_loop(0, PAIRS, expand, 0, unroll=8)

    same_before = [
        jnp.where(doc_of(first_pos + row_index - o) == docs_down, 1.0, 0.0) for o in range(1, TAPS)
    ]
    same_after = [
        jnp.where(doc_of(first_pos + row_index + o) == docs_down, 1.0, 0.0) for o in range(1, TAPS)
    ]

    arrived("conv_bias", "conv_weight")
    for i in range(TILES):
        bias[i : i + 1, :] = conv_bias[i * ROWS : (i + 1) * ROWS].reshape(1, ROWS)

    def convolve(i, carry):
        ext[i, 8:MSG, :] = conv_input[:, lanes(i)].astype(F32)
        ext[i, 0:8, :] = jnp.zeros((8, ROWS), F32)
        pre = bias[pl.ds(i, 1), :] + conv_weight[TAPS - 1 : TAPS, lanes(i)] * ext[i, 8:MSG, :]
        for o in range(1, TAPS):
            tap = conv_weight[TAPS - 1 - o : TAPS - o, lanes(i)]
            pre = pre + tap * ext[i, 8 - o : MSG - o, :] * same_before[o - 1]
        sigma = sigmoid(pre)
        act[i] = pre * sigma
        slope[i] = sigma * (1.0 + pre * (1.0 - sigma))
        return carry

    lax.fori_loop(0, TILES, convolve, 0, unroll=10)

    arrived("gate_input", "reference_out", "norm_gain")

    def gates(j, carry):
        gate = gate_input[:, lanes(j)].astype(F32)
        sigma = sigmoid(gate)
        gate_act[j] = gate * sigma
        gate_slope[j] = sigma * (1.0 + gate * (1.0 - sigma))
        for half in range(2):
            across = tall(row_of(LOG, 2 * j + half))
            gap = across.T - across
            decay[2 * j + half] = jnp.exp(jnp.where(mask[...] > 0.0, gap, -1e30))
        return carry

    lax.fori_loop(0, PAIRS, gates, 0, unroll=8)
    rim_copy.wait_recv()

    def convolve_top(i, carry):
        ext[i, 0:8, :] = rim[:, lanes(i)].astype(F32)[8:16]
        pre = bias[pl.ds(i, 1), :] + conv_weight[TAPS - 1 : TAPS, lanes(i)] * ext[i, 8:16, :]
        for o in range(1, TAPS):
            tap = conv_weight[TAPS - 1 - o : TAPS - o, lanes(i)]
            pre = pre + tap * ext[i, 8 - o : 16 - o, :] * same_before[o - 1][0:8]
        sigma = sigmoid(pre)
        act[i, 0:8, :] = pre * sigma
        slope[i, 0:8, :] = sigma * (1.0 + pre * (1.0 - sigma))
        return carry

    lax.fori_loop(0, TILES, convolve_top, 0, unroll=10)

    b_rows = act[PAIRS]
    c_rows = act[PAIRS + 1]
    b_high, b_low = split(b_rows)
    c_high, c_low = split(c_rows)
    bc[0], bc[1], bc[2], bc[3] = b_high, b_low, c_high, c_low
    bt_high, bt_low = split(b_rows.T)
    ct_high, ct_low = split(c_rows.T)
    bc[4], bc[5], bc[6], bc[7] = bt_high, bt_low, ct_high, ct_low

    def local_state(j, carry):
        part = act[j] * w_out_x[j]
        weighted[j] = part
        msg_f[j, HEAD:MSG, :] = product((bc[4], bc[5]), split(part))
        return carry

    theirs = (1 - core) * CHIPS
    mine = core * CHIPS

    def within(j, carry):
        x_pair = split(act[j])
        parts = []
        for half in range(2):
            h = 2 * j + half
            mixed = scores[...] * decay[h] * row_of(STEP, h)
            mix[h] = mixed
            parts.append(product(split(mixed), x_pair))
        inner[j] = jnp.where(first_half, parts[0], parts[1])
        return carry

    def scan(buffers, base, reverse, fill, work, afterwards, result):
        msg, near, chip, row, zin, zout, zfar, back, own, other = buffers
        is_first = core == (1 if reverse else 0)
        rank = 3 - zpos if reverse else zpos

        def ranked(place):
            return (chip_at(3 - place if reverse else place, xpos), tp)

        up = ranked(jnp.minimum(rank + 1, 3))
        far = ranked(jnp.where(rank == 0, 3, 2))
        one = jnp.ones((1, ROWS), F32)
        zero = jnp.zeros((1, ROWS), F32)

        @pl.when(rank == 0)
        def _():
            zin[...] = jnp.zeros((MSG, ROWS), F32)

        @pl.when(rank <= 1)
        def _():
            zfar[...] = jnp.zeros((ROWS, ROWS), F32)

        near_copies = []
        for q in range(CHIPS):
            fill(theirs + q, 0)
            near_copies.append(copy(msg.at[theirs + q], near.at[q], base + q, (partner, tp)))
            near_copies[-1].start()
        for q in range(CHIPS):
            fill(mine + q, 0)
        for q in range(CHIPS):
            near_copies[q].wait_recv()
            my_pass = msg[mine + q, 0:1, :]
            their_pass = near[q, 0:1, :]
            my_scale = jnp.where(is_first, their_pass, 1.0)
            their_scale = jnp.where(is_first, 1.0, my_pass)
            chip[q, HEAD:MSG, :] = (
                msg[mine + q, HEAD:MSG, :] * my_scale + near[q, HEAD:MSG, :] * their_scale
            )
            chip[q, 0:HEAD, :] = jnp.broadcast_to(my_pass * their_pass, (HEAD, ROWS))

        def place(k):
            return slice(0 if k == 0 else HEAD + k * PIECE, HEAD + (k + 1) * PIECE)

        def piece(k):
            return slice(k * PIECE, (k + 1) * PIECE)

        def body(k):
            return slice(HEAD + k * PIECE, HEAD + (k + 1) * PIECE)

        across = []
        for k in range(CHUNKS):
            sem = base + CHIPS + k * 3
            for step in (2, 1, 3):
                there = lax.rem(xpos + step, CHIPS)
                across.append(
                    copy(
                        chip.at[there, place(k)],
                        row.at[xpos, place(k)],
                        sem + step - 1,
                        (chip_at(zpos, there), tp),
                    )
                )
                across[-1].start()
        row[xpos] = chip[xpos]
        lax.fori_loop(0, SOON, work, 0)
        order = list(range(CHIPS))
        if reverse:
            order = order[::-1]
        early = SOON + jnp.where(rank == 0, 0, EARLY)
        chain = base + CHIPS + 3 * CHUNKS
        around = chain + CHUNKS
        home = around + CHUNKS

        def step_up(k):
            return copy(zout.at[place(k)], zin.at[place(k)], chain + k, up)

        def step_far(k, src):
            return copy(src, zfar.at[piece(k)], around + k, far)

        held = []
        returned = []
        for k in range(CHUNKS):
            for each in across[3 * k : 3 * k + 3]:
                each.wait_recv()
            if k == 0:
                passes = [row[x, 0:1, :] for x in order]
                scales = [one]
                for x_pass in passes:
                    scales.append(scales[-1] * x_pass)
            running = row[order[0], body(k), :]
            entering = [None]
            for x, x_pass in zip(order[1:], passes[1:]):
                entering.append(running)
                running = running * x_pass + row[x, body(k), :]
            held.append(entering)
            zout[body(k), :] = running
            if k == 0:
                zout[0:HEAD, :] = jnp.broadcast_to(scales[CHIPS], (HEAD, ROWS))

            @pl.when(rank == 2)
            def _():
                step_up(k).wait_recv()
                if k == 0:
                    zout[0:HEAD, :] = zout[0:HEAD, :] * zin[0:HEAD, :]
                zout[body(k), :] = zout[body(k), :] + zin[body(k), :] * scales[CHIPS]

            @pl.when(rank <= 2)
            def _():
                step_up(k).start()

            @pl.when(rank == 0)
            def _():
                step_far(k, zout.at[body(k)]).start()

            @pl.when(rank == 3)
            def _():
                step_far(k, zfar.at[piece(k)]).wait_recv()
                step_far(k, zfar.at[piece(k)]).start()

        lax.fori_loop(SOON, early, work, 0)
        for k in range(CHUNKS):

            @pl.when(rank == 2)
            def _():
                step_far(k, zfar.at[piece(k)]).wait_recv()

            @pl.when((rank == 1) | (rank == 3))
            def _():
                step_up(k).wait_recv()

            from_before = zin[body(k), :] + zfar[piece(k), :] * zin[0:1, :]
            for x, reached, scale in zip(order, held[k], scales):
                back[x, piece(k), :] = (
                    from_before if reached is None else reached + from_before * scale
                )
            for step in (2, 1, 3):
                there = lax.rem(xpos + step, CHIPS)
                returned.append(
                    copy(
                        back.at[there, piece(k)],
                        own.at[xpos, piece(k)],
                        home + k * 3 + step - 1,
                        (chip_at(zpos, there), tp),
                    )
                )
                returned[-1].start()
        own[xpos] = back[xpos]
        lax.fori_loop(early, PAIRS, work, 0)
        afterwards()
        last = []
        for k in range(CHUNKS):
            for each in returned[3 * k : 3 * k + 3]:
                each.wait_recv()
            for q in range(CHIPS):
                my_pass = msg[mine + q, 0:1, :]
                their_pass = near[q, 0:1, :]
                coming = own[q, piece(k), :]
                other[q, piece(k), :] = coming * jnp.where(is_first, my_pass, one) + msg[
                    mine + q, body(k), :
                ] * jnp.where(is_first, one, zero)
                result[mine + q, piece(k), :] = coming * jnp.where(
                    is_first, one, their_pass
                ) + near[q, body(k), :] * jnp.where(is_first, zero, one)
            last.append(
                copy(
                    other.at[:, piece(k)],
                    result.at[pl.ds(mine, CHIPS), piece(k)],
                    home + 3 * CHUNKS + k,
                    (partner, tp),
                )
            )
            last[-1].start()
        for each in last:
            each.wait_recv()

        def drain():
            for each in near_copies + across + returned + last:
                each.wait_send()

            @pl.when(rank <= 2)
            def _():
                for k in range(CHUNKS):
                    step_up(k).wait_send()

            @pl.when((rank == 0) | (rank == 3))
            def _():
                for k in range(CHUNKS):
                    step_far(k, zfar.at[piece(k)]).wait_send()

        return drain

    def fill_forward(j, carry):
        return local_state(j, carry)

    scores[...] = product((c_high, c_low), (b_high, b_low), (1, 1))
    forward = (msg_f, near_f, chip_f, row_f, zin_f, zout_f, zfar_f, back_f, own_f, other_f)
    drain_forward = scan(forward, 9, False, fill_forward, within, lambda: None, carried)

    sums[...] = jnp.zeros((4, ROWS, ROWS), F32)

    def outputs(j, carry):
        part = product((bc[2], bc[3]), split(carried[j])) * w_in_x[j]
        read[j] = part
        total = inner[j] + part
        inner[j] = total
        gated = total * gate_act[j]
        gained = gated * norm_gain[:, lanes(j)]
        target = reference_out[:, lanes(j)].astype(F32)
        sums[0] = sums[0] + gated * gated
        sums[1] = sums[1] + gained * target
        sums[2] = sums[2] + gained * gained
        sums[3] = sums[3] + target * target
        return carry

    lax.fori_loop(0, PAIRS, outputs, 0, unroll=8)
    square = jnp.sum(sums[0].T, axis=0, keepdims=True) / GROUP_WIDTH + 1e-05
    dot_here = jnp.sum(sums[1].T, axis=0, keepdims=True)
    self_here = jnp.sum(sums[2].T, axis=0, keepdims=True)
    ref_here = jnp.sum(sums[3].T, axis=0, keepdims=True)
    inverse = lax.rsqrt(square)
    inverse = inverse * (1.5 - 0.5 * square * inverse * inverse)
    totals[tp] = jnp.concatenate(
        [
            dot_here * inverse,
            self_here * inverse * inverse,
            ref_here,
            jnp.zeros((5, ROWS), F32),
        ],
        axis=0,
    )
    tp_copies = []
    for step in range(1, NTP):
        there = lax.rem(tp + step, NTP)
        tp_copies.append(copy(totals.at[tp], totals.at[tp], 1 + step, (ctx, there)))
        tp_copies[-1].start()
    for each in tp_copies:
        each.wait_recv()
    total = totals[0]
    for k in range(1, NTP):
        total = total + totals[k]
    mean_all = total / D_INNER
    mean_dot, mean_self, mean_ref = mean_all[0:1], mean_all[1:2], mean_all[2:3]
    norm_self = jnp.sqrt(mean_self + 1e-06)
    norm_ref = jnp.sqrt(mean_ref + 1e-06)
    cosine = mean_dot / (norm_self * norm_ref)
    distance = jnp.sqrt(mean_self - 2.0 * mean_dot + mean_ref + 1e-06)
    lane_row = lax.broadcasted_iota(jnp.int32, (1, ROWS), 1)
    harmful = jnp.where(lane_row < LBLK, labels[0], labels[1]).astype(F32)
    coef_self = -harmful * cosine / (norm_self * norm_self) + (1.0 - harmful) / distance
    coef_ref = harmful / (norm_self * norm_ref) - (1.0 - harmful) / distance
    mean_scaled = (coef_self * inverse * self_here + coef_ref * dot_here) / GROUP_WIDTH
    sums[0] = tall(coef_self * inverse * inverse).T
    sums[1] = tall(mean_scaled * inverse * inverse * inverse).T
    sums[2] = tall(coef_ref * inverse).T

    def fill_backward(j, carry):
        gain = norm_gain[:, lanes(j)]
        target = reference_out[:, lanes(j)].astype(F32)
        mixer_out = inner[j]
        gate = gate_act[j]
        gated = mixer_out * gate
        flow = gated * (sums[0] * (gain * gain) - sums[1]) + sums[2] * (gain * target)
        out_gate[:, lanes(j)] = (flow * mixer_out * gate_slope[j]).astype(BF16)
        into = flow * gate
        grad_y[j] = into
        entering = into * w_in_x[j]
        grad_in[j] = entering
        msg_b[j, HEAD:MSG, :] = product((bc[6], bc[7]), split(entering))
        return carry

    grad_scores[...] = jnp.zeros((ROWS, ROWS), F32)
    grad_b[...] = jnp.zeros((ROWS, ROWS), F32)
    grad_c[...] = jnp.zeros((ROWS, ROWS), F32)

    def halves(value):
        turned = value.T
        return (
            jnp.sum(turned[0:64], axis=0, keepdims=True),
            jnp.sum(turned[64:128], axis=0, keepdims=True),
        )

    def within_back(j, carry):
        x_pair = split(act[j])
        flow = grad_y[j]
        flow_pair = split(flow)
        by_read = halves(read[j] * flow)
        parts = []
        for half in range(2):
            h = 2 * j + half
            picked = first_half if half == 0 else jnp.logical_not(first_half)
            only = split(jnp.where(picked, flow, 0.0))
            via = product(only, x_pair, (1, 1)) * decay[h]
            step_row = row_of(STEP, h)
            grad_scores[...] = grad_scores[...] + via * step_row
            scored = via * scores[...]
            by_step = jnp.sum(scored, axis=0, keepdims=True)
            table[GSTEP, pl.ds(h, 1), :] = by_step
            across = jnp.sum((scored * step_row).T, axis=0, keepdims=True)
            table[CUM, pl.ds(h, 1), :] = across - by_step * step_row + by_read[half]
            parts.append(product(split(mix[h].T), flow_pair))
        grad_x[j] = jnp.where(first_half, parts[0], parts[1])
        grad_c[...] = grad_c[...] + product(split(grad_in[j]), split(carried[j]), (1, 1))
        return carry

    backward = (msg_b, near_b, chip_b, row_b, zin_b, zout_b, zfar_b, back_b, own_b, other_b)
    def close_scores():
        via_scores = grad_scores[...]
        grad_b[...] = product(split(via_scores.T), (bc[2], bc[3]))
        by_c = grad_c[...] + product(split(via_scores), (bc[0], bc[1]))
        grad_pre[PAIRS + 1, 0:ROWS, :] = by_c * slope[PAIRS + 1]
        rim_out[PAIRS + 1] = grad_pre[PAIRS + 1, 0:8, :]

    drain_backward = scan(
        backward, 9 + SCAN_SEMS, True, fill_backward, within_back, close_scores, adjoint
    )

    def finish(j, carry):
        coming = adjoint[j]
        coming_pair = split(coming)
        later = product((bc[0], bc[1]), coming_pair)
        grad = grad_x[j] + later * w_out_x[j]
        grad_pre[j, 0:ROWS, :] = grad * slope[j]
        rim_out[j] = grad_pre[j, 0:8, :]
        read[j] = later * act[j]
        grad_b[...] = grad_b[...] + product(split(weighted[j]), coming_pair, (1, 1))
        return carry

    lax.fori_loop(0, PAIRS, finish, 0, unroll=8)
    grad_pre[PAIRS, 0:ROWS, :] = grad_b[...] * slope[PAIRS]
    rim_out[PAIRS] = grad_pre[PAIRS, 0:8, :]
    rim_back = copy(rim_out, rim_in, 1, (before, tp))
    rim_back.start()

    def finish_rows(j, carry):
        by_weight = halves(read[j])
        table[GWEIGHT, pl.ds(2 * j, 1), :] = by_weight[0]
        table[GWEIGHT, pl.ds(2 * j + 1, 1), :] = by_weight[1]
        ended = jnp.sum(carried[j] * adjoint[j], axis=0, keepdims=True)
        table[GEND, pl.ds(2 * j, 1), :] = jnp.where(lane_row < 64, ended, 0.0)
        table[GEND, pl.ds(2 * j + 1, 1), :] = jnp.where(lane_row < 64, 0.0, ended)
        return carry

    lax.fori_loop(0, PAIRS, finish_rows, 0, unroll=8)
    grad_weight = table[GWEIGHT]
    leaving = grad_weight * table[WOUT]
    at_end = jnp.sum(leaving, axis=1, keepdims=True) + jnp.sum(
        table[GEND] * table[PASS], axis=1, keepdims=True
    )
    lane_16 = lax.broadcasted_iota(jnp.int32, (16, ROWS), 1)
    grad_cum = table[CUM] - leaving + jnp.where(lane_16 == ROWS - 1, at_end, 0.0)
    ones_lower = jnp.where(row_index >= lane_index, 1.0, 0.0).astype(BF16)
    grad_log = summed_by(grad_cum, ones_lower)
    grad_step = grad_weight * table[ENDS] + table[GSTEP]
    shifted_again = dt_raw[...] + down(dt_bias[...])
    rate_again = jnp.exp(down(a_log[...]))
    out_dt[...] = (grad_step - rate_again * grad_log) * sigmoid(shifted_again)

    drain_forward()
    rim_copy.wait_send()
    for each in tp_copies:
        each.wait_send()
    rim_back.wait_recv()
    inside = jnp.where(ctx == NCTX - 1, 0.0, 1.0)

    def spread_taps(i, carry):
        grad_pre[i, ROWS:MSG, :] = rim_in[i] * inside
        total = conv_weight[TAPS - 1 : TAPS, lanes(i)] * grad_pre[i, 0:ROWS, :]
        for o in range(1, TAPS):
            tap = conv_weight[TAPS - 1 - o : TAPS - o, lanes(i)]
            total = total + tap * grad_pre[i, o : ROWS + o, :] * same_after[o - 1]
        out_input[:, lanes(i)] = total.astype(BF16)
        return carry

    lax.fori_loop(0, TILES, spread_taps, 0, unroll=10)
    drain_backward()
    rim_back.wait_send()


def on_device(
    conv_input,
    gate_input,
    dt_raw,
    conv_weight,
    conv_bias,
    dt_bias,
    a_log,
    norm_gain,
    reference_out,
    labels,
    doc_lengths,
):
    square = (ROWS, ROWS)
    by_pair = pltpu.VMEM((PAIRS, *square), F32)
    by_tile = pltpu.VMEM((TILES, *square), F32)
    padded = pltpu.VMEM((TILES, MSG, ROWS), F32)
    one = pltpu.VMEM(square, F32)
    scans = [
        pltpu.VMEM((PAIRS, MSG, ROWS), F32),
        pltpu.VMEM((CHIPS, MSG, ROWS), F32),
        pltpu.VMEM((CHIPS, MSG, ROWS), F32),
        pltpu.VMEM((CHIPS, MSG, ROWS), F32),
        pltpu.VMEM((MSG, ROWS), F32),
        pltpu.VMEM((MSG, ROWS), F32),
        one,
        pltpu.VMEM((CHIPS, *square), F32),
        pltpu.VMEM((CHIPS, *square), F32),
        pltpu.VMEM((CHIPS, *square), F32),
    ]
    vmem = pl.BlockSpec(memory_space=pltpu.VMEM)
    far = pl.BlockSpec(memory_space=pltpu.HBM)
    held = [
        pltpu.SMEM((2,), jnp.int32),
        pltpu.SMEM((DOCS,), jnp.int32),
        pltpu.VMEM((ROWS, TILES * ROWS), BF16),
        pltpu.VMEM((ROWS, GROUP_WIDTH), BF16),
        pltpu.VMEM((16, ROWS), F32),
        pltpu.VMEM((TAPS, TILES * ROWS), F32),
        pltpu.VMEM((TILES * ROWS,), F32),
        pltpu.VMEM((1, 16), F32),
        pltpu.VMEM((1, 16), F32),
        pltpu.VMEM((1, GROUP_WIDTH), F32),
        pltpu.VMEM((ROWS, GROUP_WIDTH), BF16),
    ]
    scratch = [
        *held,
        pltpu.VMEM((TILES, ROWS), F32),
        pltpu.VMEM((16, TILES * ROWS), BF16),
        padded,
        by_tile,
        by_tile,
        by_pair,
        by_pair,
        by_pair,
        pltpu.VMEM((16, *square), F32),
        pltpu.VMEM((16, *square), F32),
        by_pair,
        by_pair,
        by_pair,
        by_pair,
        by_pair,
        by_pair,
        by_pair,
        by_pair,
        by_pair,
        padded,
        pltpu.VMEM((TILES, 8, ROWS), F32),
        pltpu.VMEM((TILES, 8, ROWS), F32),
        one,
        one,
        pltpu.VMEM((8, *square), BF16),
        pltpu.VMEM((2, PAIRS, *square), BF16),
        one,
        one,
        one,
        pltpu.VMEM((4, *square), F32),
        pltpu.VMEM((10, 16, ROWS), F32),
        pltpu.VMEM((NTP, 8, ROWS), F32),
        *scans,
        *scans,
        pltpu.SemaphoreType.DMA((9 + 2 * SCAN_SEMS,)),
        pltpu.SemaphoreType.DMA((9 + 2 * SCAN_SEMS,)),
        pltpu.SemaphoreType.DMA((11,)),
    ]
    results = pl.pallas_call(
        kernel,
        out_shape=(
            jax.ShapeDtypeStruct(conv_input.shape, BF16),
            jax.ShapeDtypeStruct(gate_input.shape, BF16),
            jax.ShapeDtypeStruct(dt_raw.shape, F32),
        ),
        in_specs=[far] * 11,
        out_specs=(vmem, vmem, vmem),
        scratch_shapes=scratch,
        compiler_params=pltpu.CompilerParams(
            collective_id=0, has_side_effects=True, vmem_limit_bytes=48 * 1024 * 1024
        ),
    )(
        pltpu.with_memory_space_constraint(labels, pltpu.HBM),
        pltpu.with_memory_space_constraint(doc_lengths, pltpu.HBM),
        pltpu.with_memory_space_constraint(conv_input, pltpu.HBM),
        pltpu.with_memory_space_constraint(gate_input, pltpu.HBM),
        pltpu.with_memory_space_constraint(dt_raw, pltpu.HBM),
        pltpu.with_memory_space_constraint(conv_weight, pltpu.HBM),
        pltpu.with_memory_space_constraint(conv_bias, pltpu.HBM),
        pltpu.with_memory_space_constraint(dt_bias.reshape(1, -1), pltpu.HBM),
        pltpu.with_memory_space_constraint(a_log.reshape(1, -1), pltpu.HBM),
        pltpu.with_memory_space_constraint(norm_gain.reshape(1, -1), pltpu.HBM),
        pltpu.with_memory_space_constraint(reference_out, pltpu.HBM),
    )
    return pl.pallas_call(
        put_out,
        out_shape=tuple(jax.ShapeDtypeStruct(each.shape, each.dtype) for each in results),
        in_specs=[vmem] * 3,
        out_specs=(far,) * 3,
        scratch_shapes=[pltpu.SemaphoreType.DMA((3,))],
        compiler_params=pltpu.CompilerParams(vmem_limit_bytes=8 * 1024 * 1024),
    )(*results)


def put_out(input_in, gate_in, dt_in, input_out, gate_out, dt_out, sem):
    moves = [
        pltpu.make_async_copy(src, dst, sem.at[place])
        for place, (src, dst) in enumerate(
            ((input_in, input_out), (gate_in, gate_out), (dt_in, dt_out))
        )
    ]
    for move in moves:
        move.start()
    for move in moves:
        move.wait()


def solution(mesh):
    in_specs = (
        P("ctx", "tp"),
        P("ctx", "tp"),
        P("tp", "ctx"),
        P(None, "tp"),
        P("tp"),
        P("tp"),
        P("tp"),
        P("tp"),
        P("ctx", "tp"),
        P("ctx"),
        P(),
    )
    out_specs = (P("ctx", "tp"), P("ctx", "tp"), P("tp", "ctx"))
    return jax.shard_map(
        on_device, mesh=mesh, in_specs=in_specs, out_specs=out_specs, check_vma=False
    )
```

```python
import functools

import jax
import jax.numpy as jnp
from jax import lax
from jax.experimental import pallas as pl
from jax.experimental.pallas import tpu as pltpu
from jax.sharding import PartitionSpec as P

HEADS = 128
HEAD_DIM = 64
STATE = 128
GROUPS = 8
TAPS = 4
LBLK = 64
DOCS = 8
D_INNER = 8192
GROUP_WIDTH = 1024
ROWS = 128
PAIRS = 8
TILES = 10
MSG = 136
HEAD = 8
CHUNKS = 4
PIECE = ROWS // CHUNKS
SOON = 4
EARLY = 4
CHIPS = 4
SCAN_SEMS = CHIPS + 9 * CHUNKS
NCTX = 32
NTP = 8
MESH = pl.DeviceIdType.MESH
F32 = jnp.float32
BF16 = jnp.bfloat16


def split(value):
    high = value.astype(BF16)
    return high, (value - high.astype(F32)).astype(BF16)


def one_pass(left, right, dims):
    return lax.dot_general(
        left, right, (((dims[0],), (dims[1],)), ((), ())), preferred_element_type=F32
    )


def product(left, right, dims=(1, 0)):
    left_high, left_low = left
    right_high, right_low = right
    return one_pass(left_high, right_high, dims) + (
        one_pass(left_high, right_low, dims) + one_pass(left_low, right_high, dims)
    )


def summed_by(value, ones):
    high = value.astype(BF16)
    rest = value - high.astype(F32)
    middle = rest.astype(BF16)
    low = (rest - middle.astype(F32)).astype(BF16)
    return one_pass(high, ones, (1, 0)) + (
        one_pass(middle, ones, (1, 0)) + one_pass(low, ones, (1, 0))
    )


def sigmoid(value):
    return 1.0 / (1.0 + jnp.exp(-value))


def tall(row):
    return jnp.broadcast_to(row, (ROWS, ROWS))


def two_heads(first, second):
    stacked = jnp.concatenate(
        [jnp.broadcast_to(first, (64, ROWS)), jnp.broadcast_to(second, (64, ROWS))], axis=0
    )
    return stacked.T


def kernel(
    labels_hbm,
    doc_lengths_hbm,
    conv_input_hbm,
    gate_input_hbm,
    dt_raw_hbm,
    conv_weight_hbm,
    conv_bias_hbm,
    dt_bias_hbm,
    a_log_hbm,
    norm_gain_hbm,
    reference_out_hbm,
    out_input,
    out_gate,
    out_dt,
    labels,
    doc_lengths,
    conv_input,
    gate_input,
    dt_raw,
    conv_weight,
    conv_bias,
    dt_bias,
    a_log,
    norm_gain,
    reference_out,
    bias,
    rim,
    ext,
    act,
    slope,
    w_out_x,
    w_in_x,
    weighted,
    decay,
    mix,
    inner,
    read,
    gate_act,
    gate_slope,
    grad_y,
    grad_in,
    carried,
    adjoint,
    grad_x,
    grad_pre,
    rim_out,
    rim_in,
    scores,
    mask,
    bc,
    arriving,
    grad_scores,
    grad_b,
    grad_c,
    sums,
    table,
    totals,
    msg_f,
    near_f,
    chip_f,
    row_f,
    zin_f,
    zout_f,
    zfar_f,
    back_f,
    own_f,
    other_f,
    msg_b,
    near_b,
    chip_b,
    row_b,
    zin_b,
    zout_b,
    zfar_b,
    back_b,
    own_b,
    other_b,
    send_sem,
    recv_sem,
    load_sem,
):
    ctx = lax.axis_index("ctx")
    tp = lax.axis_index("tp")
    core = lax.rem(ctx, 2)
    xpos = lax.rem(ctx // 2, CHIPS)
    zpos = ctx // (2 * CHIPS)
    partner = ctx + 1 - 2 * core
    after = lax.rem(ctx + 1, NCTX)
    before = lax.rem(ctx + NCTX - 1, NCTX)

    def chip_at(z, x):
        return (z * CHIPS + x) * 2 + core

    barrier = pltpu.get_barrier_semaphore()
    peers = [(after, tp), (before, tp)]
    peers.append((chip_at(lax.rem(zpos + 1, 4), xpos), tp))
    peers.append((chip_at(lax.rem(zpos + 3, 4), xpos), tp))
    for step in range(1, NTP):
        peers.append((ctx, lax.rem(tp + step, NTP)))
    for step in range(1, CHIPS):
        peers.append((chip_at(zpos, lax.rem(xpos + step, CHIPS)), tp))
    peers.append((partner, tp))
    for peer in peers:
        pl.semaphore_signal(barrier, inc=1, device_id=peer, device_id_type=MESH)

    loads = {}
    for place, (name, src, dst) in enumerate(
        (
            ("labels", labels_hbm, labels),
            ("doc_lengths", doc_lengths_hbm, doc_lengths),
            ("conv_input", conv_input_hbm, conv_input),
            ("gate_input", gate_input_hbm, gate_input),
            ("dt_raw", dt_raw_hbm, dt_raw),
            ("conv_weight", conv_weight_hbm, conv_weight),
            ("conv_bias", conv_bias_hbm, conv_bias),
            ("dt_bias", dt_bias_hbm, dt_bias),
            ("a_log", a_log_hbm, a_log),
            ("norm_gain", norm_gain_hbm, norm_gain),
            ("reference_out", reference_out_hbm, reference_out),
        )
    ):
        loads[name] = pltpu.make_async_copy(src, dst, load_sem.at[place])
        loads[name].start()

    def arrived(*which):
        for name in which:
            loads[name].wait()

    def copy(src, dst, sem, peer):
        return pltpu.make_async_remote_copy(
            src_ref=src,
            dst_ref=dst,
            send_sem=send_sem.at[sem],
            recv_sem=recv_sem.at[sem],
            device_id=peer,
            device_id_type=MESH,
        )

    row_index = lax.broadcasted_iota(jnp.int32, (ROWS, ROWS), 0)
    lane_index = lax.broadcasted_iota(jnp.int32, (ROWS, ROWS), 1)
    first_half = lane_index < 64
    first_pos = ctx * ROWS
    arrived("doc_lengths", "labels", "dt_raw", "dt_bias", "a_log")
    starts = []
    so_far = jnp.int32(0)
    for d in range(DOCS):
        starts.append(so_far)
        so_far = so_far + doc_lengths[d]

    def doc_of(position):
        found = jnp.full_like(position, -1)
        for start in starts:
            found = found + jnp.where(start <= position, 1, 0)
        return found

    docs_down = doc_of(first_pos + row_index)
    docs_across = doc_of(first_pos + lane_index)
    docs_row = docs_across[0:1, :]
    prev_doc = doc_of(jnp.full((1, ROWS), first_pos - 1, jnp.int32))
    last_doc = doc_of(jnp.full((1, ROWS), first_pos + ROWS - 1, jnp.int32))
    mask[...] = jnp.where((row_index >= lane_index) & (docs_down == docs_across), 1.0, 0.0)
    keep_out = jnp.where(docs_row == last_doc, 1.0, 0.0)
    keep_in = jnp.where(docs_row == prev_doc, 1.0, 0.0)
    through = jnp.where(prev_doc == last_doc, 1.0, 0.0)

    eye = (
        lax.broadcasted_iota(jnp.int32, (16, 16), 0) == lax.broadcasted_iota(jnp.int32, (16, 16), 1)
    )

    def down(row):
        return jnp.sum(jnp.where(eye, jnp.broadcast_to(row, (16, 16)), 0.0), axis=1, keepdims=True)

    shifted = dt_raw[...] + down(dt_bias[...])
    rate = jnp.exp(down(a_log[...]))
    small = jnp.exp(-jnp.abs(shifted))
    step_size = jnp.maximum(shifted, 0.0) + jnp.log1p(small)
    ones_upper = jnp.where(row_index <= lane_index, 1.0, 0.0).astype(BF16)
    log_cumul = summed_by(-rate * step_size, ones_upper)
    log_end = log_cumul[:, ROWS - 1 : ROWS]
    ends = jnp.exp(log_end - log_cumul) * keep_out
    w_out = ends * step_size
    w_in = jnp.exp(log_cumul) * keep_in
    passing = jnp.broadcast_to(jnp.exp(log_end), (16, ROWS)) * through
    LOG, STEP, ENDS, WOUT, WIN, PASS, CUM, GSTEP, GWEIGHT, GEND = range(10)
    table[LOG] = log_cumul
    table[STEP] = step_size
    table[ENDS] = ends
    table[WOUT] = w_out
    table[WIN] = w_in
    table[PASS] = passing

    arrived("conv_input")
    pl.semaphore_wait(barrier, len(peers))
    rim_copy = copy(conv_input.at[ROWS - 16 : ROWS], rim, 0, (after, tp))
    rim_copy.start()

    def lanes(i):
        return pl.ds(pl.multiple_of(i * ROWS, ROWS), ROWS)

    def row_of(which, h):
        return table[which, pl.ds(h, 1), :]

    def expand(j, carry):
        w_out_x[j] = two_heads(row_of(WOUT, 2 * j), row_of(WOUT, 2 * j + 1))
        w_in_x[j] = two_heads(row_of(WIN, 2 * j), row_of(WIN, 2 * j + 1))
        lane_row = lax.broadcasted_iota(jnp.int32, (1, ROWS), 1)
        pass_row = jnp.where(lane_row < 64, row_of(PASS, 2 * j), row_of(PASS, 2 * j + 1))
        pass_rows = jnp.broadcast_to(pass_row, (8, ROWS))
        msg_f[j, 0:HEAD, :] = pass_rows
        msg_b[j, 0:HEAD, :] = pass_rows
        return carry

    lax.fori_loop(0, PAIRS, expand, 0, unroll=8)

    same_before = [
        jnp.where(doc_of(first_pos + row_index - o) == docs_down, 1.0, 0.0) for o in range(1, TAPS)
    ]
    same_after = [
        jnp.where(doc_of(first_pos + row_index + o) == docs_down, 1.0, 0.0) for o in range(1, TAPS)
    ]

    arrived("conv_bias", "conv_weight")
    for i in range(TILES):
        bias[i : i + 1, :] = conv_bias[i * ROWS : (i + 1) * ROWS].reshape(1, ROWS)

    def convolve(i, carry):
        ext[i, 8:MSG, :] = conv_input[:, lanes(i)].astype(F32)
        ext[i, 0:8, :] = jnp.zeros((8, ROWS), F32)
        pre = bias[pl.ds(i, 1), :] + conv_weight[TAPS - 1 : TAPS, lanes(i)] * ext[i, 8:MSG, :]
        for o in range(1, TAPS):
            tap = conv_weight[TAPS - 1 - o : TAPS - o, lanes(i)]
            pre = pre + tap * ext[i, 8 - o : MSG - o, :] * same_before[o - 1]
        sigma = sigmoid(pre)
        act[i] = pre * sigma
        slope[i] = sigma * (1.0 + pre * (1.0 - sigma))
        return carry

    lax.fori_loop(0, TILES, convolve, 0, unroll=10)

    arrived("gate_input", "reference_out", "norm_gain")

    sums[3] = jnp.zeros((ROWS, ROWS), F32)

    def gates(j, carry):
        target = reference_out[:, lanes(j)].astype(F32)
        sums[3] = sums[3] + target * target
        gate = gate_input[:, lanes(j)].astype(F32)
        sigma = sigmoid(gate)
        gate_act[j] = gate * sigma
        gate_slope[j] = sigma * (1.0 + gate * (1.0 - sigma))
        for half in range(2):
            across = tall(row_of(LOG, 2 * j + half))
            gap = across.T - across
            decay[2 * j + half] = jnp.exp(jnp.where(mask[...] > 0.0, gap, -1e30))
        return carry

    lax.fori_loop(0, PAIRS, gates, 0, unroll=8)
    rim_copy.wait_recv()

    def convolve_top(i, carry):
        ext[i, 0:8, :] = rim[:, lanes(i)].astype(F32)[8:16]
        pre = bias[pl.ds(i, 1), :] + conv_weight[TAPS - 1 : TAPS, lanes(i)] * ext[i, 8:16, :]
        for o in range(1, TAPS):
            tap = conv_weight[TAPS - 1 - o : TAPS - o, lanes(i)]
            pre = pre + tap * ext[i, 8 - o : 16 - o, :] * same_before[o - 1][0:8]
        sigma = sigmoid(pre)
        act[i, 0:8, :] = pre * sigma
        slope[i, 0:8, :] = sigma * (1.0 + pre * (1.0 - sigma))
        return carry

    lax.fori_loop(0, TILES, convolve_top, 0, unroll=10)

    b_rows = act[PAIRS]
    c_rows = act[PAIRS + 1]
    b_high, b_low = split(b_rows)
    c_high, c_low = split(c_rows)
    bc[0], bc[1], bc[2], bc[3] = b_high, b_low, c_high, c_low
    bt_high, bt_low = split(b_rows.T)
    ct_high, ct_low = split(c_rows.T)
    bc[4], bc[5], bc[6], bc[7] = bt_high, bt_low, ct_high, ct_low

    def local_state(j, carry):
        part = act[j] * w_out_x[j]
        weighted[j] = part
        msg_f[j, HEAD:MSG, :] = product((bc[4], bc[5]), split(part))
        return carry

    theirs = (1 - core) * CHIPS
    mine = core * CHIPS

    def within(j, carry):
        x_pair = split(act[j])
        parts = []
        for half in range(2):
            h = 2 * j + half
            mixed = scores[...] * decay[h] * row_of(STEP, h)
            mix[h] = mixed
            parts.append(product(split(mixed), x_pair))
        inner[j] = jnp.where(first_half, parts[0], parts[1])
        return carry

    def scan(buffers, base, reverse, fill, work, afterwards, result):
        msg, near, chip, row, zin, zout, zfar, back, own, other = buffers
        is_first = core == (1 if reverse else 0)
        rank = 3 - zpos if reverse else zpos

        def ranked(place):
            return (chip_at(3 - place if reverse else place, xpos), tp)

        up = ranked(jnp.minimum(rank + 1, 3))
        far = ranked(jnp.where(rank == 0, 3, 2))
        one = jnp.ones((1, ROWS), F32)
        zero = jnp.zeros((1, ROWS), F32)

        @pl.when(rank == 0)
        def _():
            zin[...] = jnp.zeros((MSG, ROWS), F32)

        @pl.when(rank <= 1)
        def _():
            zfar[...] = jnp.zeros((ROWS, ROWS), F32)

        near_copies = []
        for q in range(CHIPS):
            fill(theirs + q, 0)
            near_copies.append(copy(msg.at[theirs + q], near.at[q], base + q, (partner, tp)))
            near_copies[-1].start()
        for q in range(CHIPS):
            fill(mine + q, 0)
        for q in range(CHIPS):
            near_copies[q].wait_recv()
            my_pass = msg[mine + q, 0:1, :]
            their_pass = near[q, 0:1, :]
            my_scale = jnp.where(is_first, their_pass, 1.0)
            their_scale = jnp.where(is_first, 1.0, my_pass)
            chip[q, HEAD:MSG, :] = (
                msg[mine + q, HEAD:MSG, :] * my_scale + near[q, HEAD:MSG, :] * their_scale
            )
            chip[q, 0:HEAD, :] = jnp.broadcast_to(my_pass * their_pass, (HEAD, ROWS))

        def place(k):
            return slice(0 if k == 0 else HEAD + k * PIECE, HEAD + (k + 1) * PIECE)

        def piece(k):
            return slice(k * PIECE, (k + 1) * PIECE)

        def body(k):
            return slice(HEAD + k * PIECE, HEAD + (k + 1) * PIECE)

        across = []
        for k in range(CHUNKS):
            sem = base + CHIPS + k * 3
            for step in (2, 1, 3):
                there = lax.rem(xpos + step, CHIPS)
                across.append(
                    copy(
                        chip.at[there, place(k)],
                        row.at[xpos, place(k)],
                        sem + step - 1,
                        (chip_at(zpos, there), tp),
                    )
                )
                across[-1].start()
        row[xpos] = chip[xpos]
        lax.fori_loop(0, SOON, work, 0)
        order = list(range(CHIPS))
        if reverse:
            order = order[::-1]
        early = SOON + jnp.where(rank == 0, 0, EARLY)
        chain = base + CHIPS + 3 * CHUNKS
        around = chain + CHUNKS
        home = around + CHUNKS

        def step_up(k):
            return copy(zout.at[place(k)], zin.at[place(k)], chain + k, up)

        def step_far(k, src):
            return copy(src, zfar.at[piece(k)], around + k, far)

        held = []
        returned = []
        for k in range(CHUNKS):
            for each in across[3 * k : 3 * k + 3]:
                each.wait_recv()
            if k == 0:
                passes = [row[x, 0:1, :] for x in order]
                scales = [one]
                for x_pass in passes:
                    scales.append(scales[-1] * x_pass)
            running = row[order[0], body(k), :]
            entering = [None]
            for x, x_pass in zip(order[1:], passes[1:]):
                entering.append(running)
                running = running * x_pass + row[x, body(k), :]
            held.append(entering)
            zout[body(k), :] = running
            if k == 0:
                zout[0:HEAD, :] = jnp.broadcast_to(scales[CHIPS], (HEAD, ROWS))

            @pl.when(rank == 2)
            def _():
                step_up(k).wait_recv()
                if k == 0:
                    zout[0:HEAD, :] = zout[0:HEAD, :] * zin[0:HEAD, :]
                zout[body(k), :] = zout[body(k), :] + zin[body(k), :] * scales[CHIPS]

            @pl.when(rank <= 2)
            def _():
                step_up(k).start()

            @pl.when(rank == 0)
            def _():
                step_far(k, zout.at[body(k)]).start()

            @pl.when(rank == 3)
            def _():
                step_far(k, zfar.at[piece(k)]).wait_recv()
                step_far(k, zfar.at[piece(k)]).start()

        lax.fori_loop(SOON, early, work, 0)
        for k in range(CHUNKS):

            @pl.when(rank == 2)
            def _():
                step_far(k, zfar.at[piece(k)]).wait_recv()

            @pl.when((rank == 1) | (rank == 3))
            def _():
                step_up(k).wait_recv()

            from_before = zin[body(k), :] + zfar[piece(k), :] * zin[0:1, :]
            for x, reached, scale in zip(order, held[k], scales):
                back[x, piece(k), :] = (
                    from_before if reached is None else reached + from_before * scale
                )
            for step in (2, 1, 3):
                there = lax.rem(xpos + step, CHIPS)
                returned.append(
                    copy(
                        back.at[there, piece(k)],
                        own.at[xpos, piece(k)],
                        home + k * 3 + step - 1,
                        (chip_at(zpos, there), tp),
                    )
                )
                returned[-1].start()
        own[xpos] = back[xpos]
        lax.fori_loop(early, PAIRS, work, 0)
        afterwards()
        last = []
        for k in range(CHUNKS):
            for each in returned[3 * k : 3 * k + 3]:
                each.wait_recv()
            for q in range(CHIPS):
                my_pass = msg[mine + q, 0:1, :]
                their_pass = near[q, 0:1, :]
                coming = own[q, piece(k), :]
                other[q, piece(k), :] = coming * jnp.where(is_first, my_pass, one) + msg[
                    mine + q, body(k), :
                ] * jnp.where(is_first, one, zero)
                result[mine + q, piece(k), :] = coming * jnp.where(
                    is_first, one, their_pass
                ) + near[q, body(k), :] * jnp.where(is_first, zero, one)
            last.append(
                copy(
                    other.at[:, piece(k)],
                    result.at[pl.ds(mine, CHIPS), piece(k)],
                    home + 3 * CHUNKS + k,
                    (partner, tp),
                )
            )
            last[-1].start()
        for each in last:
            each.wait_recv()

        def drain():
            for each in near_copies + across + returned + last:
                each.wait_send()

            @pl.when(rank <= 2)
            def _():
                for k in range(CHUNKS):
                    step_up(k).wait_send()

            @pl.when((rank == 0) | (rank == 3))
            def _():
                for k in range(CHUNKS):
                    step_far(k, zfar.at[piece(k)]).wait_send()

        return drain

    def fill_forward(j, carry):
        return local_state(j, carry)

    scores[...] = product((c_high, c_low), (b_high, b_low), (1, 1))
    forward = (msg_f, near_f, chip_f, row_f, zin_f, zout_f, zfar_f, back_f, own_f, other_f)

    def close_targets():
        table[LOG, 0:1, :] = jnp.sum(sums[3].T, axis=0, keepdims=True)

    drain_forward = scan(forward, 9, False, fill_forward, within, close_targets, carried)

    sums[0:3] = jnp.zeros((3, ROWS, ROWS), F32)

    def outputs(j, carry):
        part = product((bc[2], bc[3]), split(carried[j])) * w_in_x[j]
        read[j] = part
        total = inner[j] + part
        inner[j] = total
        gated = total * gate_act[j]
        gained = gated * norm_gain[:, lanes(j)]
        target = reference_out[:, lanes(j)].astype(F32)
        sums[0] = sums[0] + gated * gated
        sums[1] = sums[1] + gained * target
        sums[2] = sums[2] + gained * gained
        return carry

    lax.fori_loop(0, PAIRS, outputs, 0, unroll=8)
    square = jnp.sum(sums[0].T, axis=0, keepdims=True) / GROUP_WIDTH + 1e-05
    dot_here = jnp.sum(sums[1].T, axis=0, keepdims=True)
    self_here = jnp.sum(sums[2].T, axis=0, keepdims=True)
    inverse = lax.rsqrt(square)
    inverse = inverse * (1.5 - 0.5 * square * inverse * inverse)
    totals[tp] = jnp.concatenate(
        [
            dot_here * inverse,
            self_here * inverse * inverse,
            table[LOG, 0:1, :],
            jnp.zeros((5, ROWS), F32),
        ],
        axis=0,
    )
    tp_copies = []
    for step in range(1, NTP):
        there = lax.rem(tp + step, NTP)
        tp_copies.append(copy(totals.at[tp], totals.at[tp], 1 + step, (ctx, there)))
        tp_copies[-1].start()
    for each in tp_copies:
        each.wait_recv()
    total = totals[0]
    for k in range(1, NTP):
        total = total + totals[k]
    mean_all = total / D_INNER
    mean_dot, mean_self, mean_ref = mean_all[0:1], mean_all[1:2], mean_all[2:3]
    norm_self = jnp.sqrt(mean_self + 1e-06)
    norm_ref = jnp.sqrt(mean_ref + 1e-06)
    cosine = mean_dot / (norm_self * norm_ref)
    distance = jnp.sqrt(mean_self - 2.0 * mean_dot + mean_ref + 1e-06)
    lane_row = lax.broadcasted_iota(jnp.int32, (1, ROWS), 1)
    harmful = jnp.where(lane_row < LBLK, labels[0], labels[1]).astype(F32)
    coef_self = -harmful * cosine / (norm_self * norm_self) + (1.0 - harmful) / distance
    coef_ref = harmful / (norm_self * norm_ref) - (1.0 - harmful) / distance
    mean_scaled = (coef_self * inverse * self_here + coef_ref * dot_here) / GROUP_WIDTH
    sums[0] = tall(coef_self * inverse * inverse).T
    sums[1] = tall(mean_scaled * inverse * inverse * inverse).T
    sums[2] = tall(coef_ref * inverse).T

    def fill_backward(j, carry):
        gain = norm_gain[:, lanes(j)]
        target = reference_out[:, lanes(j)].astype(F32)
        mixer_out = inner[j]
        gate = gate_act[j]
        gated = mixer_out * gate
        flow = gated * (sums[0] * (gain * gain) - sums[1]) + sums[2] * (gain * target)
        out_gate[:, lanes(j)] = (flow * mixer_out * gate_slope[j]).astype(BF16)
        into = flow * gate
        grad_y[j] = into
        entering = into * w_in_x[j]
        grad_in[j] = entering
        msg_b[j, HEAD:MSG, :] = product((bc[6], bc[7]), split(entering))
        return carry

    grad_scores[...] = jnp.zeros((ROWS, ROWS), F32)
    grad_b[...] = jnp.zeros((ROWS, ROWS), F32)
    grad_c[...] = jnp.zeros((ROWS, ROWS), F32)

    def halves(value):
        turned = value.T
        return (
            jnp.sum(turned[0:64], axis=0, keepdims=True),
            jnp.sum(turned[64:128], axis=0, keepdims=True),
        )

    def within_back(j, carry):
        x_pair = split(act[j])
        flow = grad_y[j]
        flow_pair = split(flow)
        by_read = halves(read[j] * flow)
        parts = []
        for half in range(2):
            h = 2 * j + half
            picked = first_half if half == 0 else jnp.logical_not(first_half)
            only = split(jnp.where(picked, flow, 0.0))
            via = product(only, x_pair, (1, 1)) * decay[h]
            step_row = row_of(STEP, h)
            grad_scores[...] = grad_scores[...] + via * step_row
            scored = via * scores[...]
            by_step = jnp.sum(scored, axis=0, keepdims=True)
            table[GSTEP, pl.ds(h, 1), :] = by_step
            across = jnp.sum((scored * step_row).T, axis=0, keepdims=True)
            table[CUM, pl.ds(h, 1), :] = across - by_step * step_row + by_read[half]
            parts.append(product(split(mix[h].T), flow_pair))
        grad_x[j] = jnp.where(first_half, parts[0], parts[1])
        grad_c[...] = grad_c[...] + product(split(grad_in[j]), split(carried[j]), (1, 1))
        return carry

    backward = (msg_b, near_b, chip_b, row_b, zin_b, zout_b, zfar_b, back_b, own_b, other_b)
    def close_scores():
        via_scores = grad_scores[...]
        grad_b[...] = product(split(via_scores.T), (bc[2], bc[3]))
        by_c = grad_c[...] + product(split(via_scores), (bc[0], bc[1]))
        grad_pre[PAIRS + 1, 0:ROWS, :] = by_c * slope[PAIRS + 1]
        rim_out[PAIRS + 1] = grad_pre[PAIRS + 1, 0:8, :]

    drain_backward = scan(
        backward, 9 + SCAN_SEMS, True, fill_backward, within_back, close_scores, adjoint
    )

    def finish(j, carry):
        coming = adjoint[j]
        coming_pair = split(coming)
        later = product((bc[0], bc[1]), coming_pair)
        grad = grad_x[j] + later * w_out_x[j]
        grad_pre[j, 0:ROWS, :] = grad * slope[j]
        rim_out[j] = grad_pre[j, 0:8, :]
        read[j] = later * act[j]
        grad_b[...] = grad_b[...] + product(split(weighted[j]), coming_pair, (1, 1))
        return carry

    lax.fori_loop(0, PAIRS, finish, 0, unroll=8)
    grad_pre[PAIRS, 0:ROWS, :] = grad_b[...] * slope[PAIRS]
    rim_out[PAIRS] = grad_pre[PAIRS, 0:8, :]
    rim_back = copy(rim_out, rim_in, 1, (before, tp))
    rim_back.start()

    def finish_rows(j, carry):
        by_weight = halves(read[j])
        table[GWEIGHT, pl.ds(2 * j, 1), :] = by_weight[0]
        table[GWEIGHT, pl.ds(2 * j + 1, 1), :] = by_weight[1]
        ended = jnp.sum(carried[j] * adjoint[j], axis=0, keepdims=True)
        table[GEND, pl.ds(2 * j, 1), :] = jnp.where(lane_row < 64, ended, 0.0)
        table[GEND, pl.ds(2 * j + 1, 1), :] = jnp.where(lane_row < 64, 0.0, ended)
        return carry

    lax.fori_loop(0, PAIRS, finish_rows, 0, unroll=8)
    grad_weight = table[GWEIGHT]
    leaving = grad_weight * table[WOUT]
    at_end = jnp.sum(leaving, axis=1, keepdims=True) + jnp.sum(
        table[GEND] * table[PASS], axis=1, keepdims=True
    )
    lane_16 = lax.broadcasted_iota(jnp.int32, (16, ROWS), 1)
    grad_cum = table[CUM] - leaving + jnp.where(lane_16 == ROWS - 1, at_end, 0.0)
    ones_lower = jnp.where(row_index >= lane_index, 1.0, 0.0).astype(BF16)
    grad_log = summed_by(grad_cum, ones_lower)
    grad_step = grad_weight * table[ENDS] + table[GSTEP]
    shifted_again = dt_raw[...] + down(dt_bias[...])
    rate_again = jnp.exp(down(a_log[...]))
    out_dt[...] = (grad_step - rate_again * grad_log) * sigmoid(shifted_again)

    drain_forward()
    rim_copy.wait_send()
    for each in tp_copies:
        each.wait_send()
    rim_back.wait_recv()
    inside = jnp.where(ctx == NCTX - 1, 0.0, 1.0)

    def spread_taps(i, carry):
        grad_pre[i, ROWS:MSG, :] = rim_in[i] * inside
        total = conv_weight[TAPS - 1 : TAPS, lanes(i)] * grad_pre[i, 0:ROWS, :]
        for o in range(1, TAPS):
            tap = conv_weight[TAPS - 1 - o : TAPS - o, lanes(i)]
            total = total + tap * grad_pre[i, o : ROWS + o, :] * same_after[o - 1]
        out_input[:, lanes(i)] = total.astype(BF16)
        return carry

    lax.fori_loop(0, TILES, spread_taps, 0, unroll=10)
    drain_backward()
    rim_back.wait_send()


def on_device(
    conv_input,
    gate_input,
    dt_raw,
    conv_weight,
    conv_bias,
    dt_bias,
    a_log,
    norm_gain,
    reference_out,
    labels,
    doc_lengths,
):
    square = (ROWS, ROWS)
    by_pair = pltpu.VMEM((PAIRS, *square), F32)
    by_tile = pltpu.VMEM((TILES, *square), F32)
    padded = pltpu.VMEM((TILES, MSG, ROWS), F32)
    one = pltpu.VMEM(square, F32)
    scans = [
        pltpu.VMEM((PAIRS, MSG, ROWS), F32),
        pltpu.VMEM((CHIPS, MSG, ROWS), F32),
        pltpu.VMEM((CHIPS, MSG, ROWS), F32),
        pltpu.VMEM((CHIPS, MSG, ROWS), F32),
        pltpu.VMEM((MSG, ROWS), F32),
        pltpu.VMEM((MSG, ROWS), F32),
        one,
        pltpu.VMEM((CHIPS, *square), F32),
        pltpu.VMEM((CHIPS, *square), F32),
        pltpu.VMEM((CHIPS, *square), F32),
    ]
    vmem = pl.BlockSpec(memory_space=pltpu.VMEM)
    far = pl.BlockSpec(memory_space=pltpu.HBM)
    held = [
        pltpu.SMEM((2,), jnp.int32),
        pltpu.SMEM((DOCS,), jnp.int32),
        pltpu.VMEM((ROWS, TILES * ROWS), BF16),
        pltpu.VMEM((ROWS, GROUP_WIDTH), BF16),
        pltpu.VMEM((16, ROWS), F32),
        pltpu.VMEM((TAPS, TILES * ROWS), F32),
        pltpu.VMEM((TILES * ROWS,), F32),
        pltpu.VMEM((1, 16), F32),
        pltpu.VMEM((1, 16), F32),
        pltpu.VMEM((1, GROUP_WIDTH), F32),
        pltpu.VMEM((ROWS, GROUP_WIDTH), BF16),
    ]
    scratch = [
        *held,
        pltpu.VMEM((TILES, ROWS), F32),
        pltpu.VMEM((16, TILES * ROWS), BF16),
        padded,
        by_tile,
        by_tile,
        by_pair,
        by_pair,
        by_pair,
        pltpu.VMEM((16, *square), F32),
        pltpu.VMEM((16, *square), F32),
        by_pair,
        by_pair,
        by_pair,
        by_pair,
        by_pair,
        by_pair,
        by_pair,
        by_pair,
        by_pair,
        padded,
        pltpu.VMEM((TILES, 8, ROWS), F32),
        pltpu.VMEM((TILES, 8, ROWS), F32),
        one,
        one,
        pltpu.VMEM((8, *square), BF16),
        pltpu.VMEM((2, PAIRS, *square), BF16),
        one,
        one,
        one,
        pltpu.VMEM((4, *square), F32),
        pltpu.VMEM((10, 16, ROWS), F32),
        pltpu.VMEM((NTP, 8, ROWS), F32),
        *scans,
        *scans,
        pltpu.SemaphoreType.DMA((9 + 2 * SCAN_SEMS,)),
        pltpu.SemaphoreType.DMA((9 + 2 * SCAN_SEMS,)),
        pltpu.SemaphoreType.DMA((11,)),
    ]
    results = pl.pallas_call(
        kernel,
        out_shape=(
            jax.ShapeDtypeStruct(conv_input.shape, BF16),
            jax.ShapeDtypeStruct(gate_input.shape, BF16),
            jax.ShapeDtypeStruct(dt_raw.shape, F32),
        ),
        in_specs=[far] * 11,
        out_specs=(vmem, vmem, vmem),
        scratch_shapes=scratch,
        compiler_params=pltpu.CompilerParams(
            collective_id=0, has_side_effects=True, vmem_limit_bytes=48 * 1024 * 1024
        ),
    )(
        pltpu.with_memory_space_constraint(labels, pltpu.HBM),
        pltpu.with_memory_space_constraint(doc_lengths, pltpu.HBM),
        pltpu.with_memory_space_constraint(conv_input, pltpu.HBM),
        pltpu.with_memory_space_constraint(gate_input, pltpu.HBM),
        pltpu.with_memory_space_constraint(dt_raw, pltpu.HBM),
        pltpu.with_memory_space_constraint(conv_weight, pltpu.HBM),
        pltpu.with_memory_space_constraint(conv_bias, pltpu.HBM),
        pltpu.with_memory_space_constraint(dt_bias.reshape(1, -1), pltpu.HBM),
        pltpu.with_memory_space_constraint(a_log.reshape(1, -1), pltpu.HBM),
        pltpu.with_memory_space_constraint(norm_gain.reshape(1, -1), pltpu.HBM),
        pltpu.with_memory_space_constraint(reference_out, pltpu.HBM),
    )
    return pl.pallas_call(
        put_out,
        out_shape=tuple(jax.ShapeDtypeStruct(each.shape, each.dtype) for each in results),
        in_specs=[vmem] * 3,
        out_specs=(far,) * 3,
        scratch_shapes=[pltpu.SemaphoreType.DMA((3,))],
        compiler_params=pltpu.CompilerParams(vmem_limit_bytes=8 * 1024 * 1024),
    )(*results)


def put_out(input_in, gate_in, dt_in, input_out, gate_out, dt_out, sem):
    moves = [
        pltpu.make_async_copy(src, dst, sem.at[place])
        for place, (src, dst) in enumerate(
            ((input_in, input_out), (gate_in, gate_out), (dt_in, dt_out))
        )
    ]
    for move in moves:
        move.start()
    for move in moves:
        move.wait()


def solution(mesh):
    in_specs = (
        P("ctx", "tp"),
        P("ctx", "tp"),
        P("tp", "ctx"),
        P(None, "tp"),
        P("tp"),
        P("tp"),
        P("tp"),
        P("tp"),
        P("ctx", "tp"),
        P("ctx"),
        P(),
    )
    out_specs = (P("ctx", "tp"), P("ctx", "tp"), P("tp", "ctx"))
    return jax.shard_map(
        on_device, mesh=mesh, in_specs=in_specs, out_specs=out_specs, check_vma=False
    )
```
